32 devices in a mesh: chan: 8 (over y, x, core), facet: 4 (over z).
Axes of the slice: x: 2, y: 2, z: 4, core: 2. Of those that a mesh axis runs over, the one named last changes fastest.
Arguments:
- x_init: float32 [128, 256, 2048], P('chan', 'facet'), may hold values from 0 to 2
- u_init: float32 [128, 2, 256, 2048], P('chan', None, 'facet')
- v_init: float32 [128, 32, 2, 128], P('chan'), may hold values from -4 to 4
- observed: float32 [128, 32, 2, 128], P('chan'), may hold values from -6 to 6
- tiles: bfloat16 [128, 32, 2, 128, 128], P('chan'), may hold values from -0.375 to 0.375
- pattern: int32 [128, 32, 2], P('chan'), may hold values from 0 to 4095
- counts: int32 [128], P('chan'), may hold values from 1 to 32, as said below
- facet_bounds: int32 [4, 2], replicated, may hold values from 0 to 256, as said below
Outputs:
- image: float32 [128, 256, 2048], P('chan', 'facet')
- prior_dual: float32 [128, 2, 256, 2048], P('chan', None, 'facet')
- data_dual: float32 [128, 32, 2, 128], P('chan')
The draws below stay inside these ranges and needn't reach their ends.
Inputs may be any that keep to these rules, and one draw needn't show every extreme that they name: `counts`: channels 128 - 128/4 to 127 hold 32 live blocks each; the others hold fewer than half of 32, and at least one. `facet_bounds`: facet 0 starts at row 0 and the last facet ends at row 256; facets are in order, and each facet after the first starts one to 16 rows before the previous one ends, so every row lies in one or two facets.
All inputs are finite; a program needn't handle non-finite values.
Results may differ from the reference program's by a relative error of at most 0.0032.
Values sent between devices are 32-bit elements; how exact they have to be, the bound alone decides.
No kernel may reach another device: no remote copies, remote signals or barrier semaphores. Data moves between devices by JAX's collectives and lax.ppermute only.
A program may use at most 256 MiB of HBM per device.

```python
import math
import jax
import jax.numpy as jnp
from jax import lax

C = 128
W = 2048
BLK = 128
VB = 32
K = 2
ITERS = 2
H = 256
NF = 4
KB = 16


def draw_u_init(key, part):
    chan_scale = 10.0 ** (jnp.arange(C, dtype=jnp.float32) / (C - 1))
    split_keys = jax.random.split(key, 2)
    values = jax.random.normal(split_keys[0], (C, 2, H, W), jnp.float32)
    row_scale = jnp.exp(jax.random.uniform(split_keys[1], (1, 2, H, 1), jnp.float32, -4.5, 0.0))
    return values * row_scale * chan_scale[:, None, None, None]


def draw_counts(key, part):
    highest = max(2, VB // 2)
    light = jax.random.randint(key, (C,), 1, highest)
    heavy = jnp.arange(C) >= C - C // 4
    return jnp.where(heavy, VB, light).astype(jnp.int32)


def draw_facet_bounds(key, part):
    split_keys = jax.random.split(key)
    spread = H // (4 * NF)
    edges = jnp.arange(NF + 1) * (H // NF) + jax.random.randint(split_keys[0], (NF + 1,), -spread, spread + 1)
    edges = edges.at[0].set(0).at[NF].set(H)
    margin = jax.random.randint(split_keys[1], (NF,), 1, spread + 1)
    lower = jnp.maximum(edges[:NF] - margin, 0)
    return jnp.stack([lower, edges[1:]], axis=1).astype(jnp.int32)


def place_ends(result, key, smallest, largest):
    place = [jax.random.randint(jax.random.fold_in(key, axis), (), 0, length) for axis, length in enumerate(result.shape)]
    main_axis = result.shape.index(max(result.shape))
    beside = place[:main_axis] + [(place[main_axis] + 1) % result.shape[main_axis]] + place[main_axis + 1:]
    return result.at[tuple(place)].set(smallest).at[tuple(beside)].set(largest)


def levels(stream_key, shape, cuts, low, high):
    def one(axis_at, parts):
        draws = jax.random.uniform(jax.random.fold_in(jax.random.fold_in(stream_key, 6), axis_at), (parts,), jnp.float32, low / len(cuts), high / len(cuts))
        return jnp.repeat(jnp.exp(draws), shape[axis_at] // parts).reshape((-1,) + (1,) * (len(shape) - axis_at - 1))

    loudness = one(*cuts[0])
    for cut in cuts[1:]:
        loudness = loudness * one(*cut)
    return loudness


def bell_draw(rng, dims, width, most, pieces=(), held_as=jnp.bfloat16):
    values = jax.random.normal(rng, dims, jnp.float32) * width
    if len(pieces) > 0:
        values = levels(rng, dims, pieces, -0.22, 0.18) * values
    return jnp.clip(values, min=-most, max=most).astype(held_as)


def setup_inputs(seed: int = 0) -> dict:
    key_of = jax.random.split(jax.random.key(seed), 9)
    x_init = jnp.clip(2.0 * jax.random.uniform(key_of[0], (C, H, W), jnp.float32) ** levels(key_of[0], (C, H, W), ((0, 8), (1, 4)), -0.2, 0.2), 0.0, 2.0)
    u_init = draw_u_init(jax.random.fold_in(key_of[8], 71), 0)
    v_init = bell_draw(key_of[2], (C, VB, 2, BLK), 0.5, 4.0, ((0, 8),), jnp.float32)
    observed = bell_draw(key_of[3], (C, VB, 2, BLK), 1.0, 6.0, ((0, 8),), jnp.float32)
    tiles = bell_draw(key_of[4], (C, VB, K, BLK, BLK), (K * BLK) ** -0.5, 0.375, ((0, 8),))
    pattern = place_ends(jax.random.randint(key_of[5], (C, VB, K), 0, H * KB), jax.random.fold_in(key_of[5], 1), 0, (H * KB) - 1).astype(jnp.int32)
    counts = draw_counts(jax.random.fold_in(key_of[8], 71), 0)
    facet_bounds = draw_facet_bounds(jax.random.fold_in(key_of[8], 71), 0)
    return {"x_init": x_init, "u_init": u_init, "v_init": v_init, "observed": observed, "tiles": tiles, "pattern": pattern, "counts": counts, "facet_bounds": facet_bounds}


STEP_PRIMAL = 0.5
STEP_PRIOR = 0.5
STEP_DATA = 1.0
RADIUS = 12.0
ROOT_HALF = 0.7071067811865476

def dft_table(extent, tile_side):
    column = jnp.arange(2 * extent, dtype=jnp.int32)
    is_sine = column // tile_side % 2
    frequency = column // (2 * tile_side) * tile_side + column % tile_side
    row_index = jnp.arange(extent, dtype=jnp.int32)
    phases = row_index[:, None] * frequency[None, :] % extent
    angles = phases.astype(jnp.float32) * (2.0 * math.pi / extent)
    values = jnp.where(is_sine[None, :] == 0, jnp.cos(angles), -jnp.sin(angles))
    return (values / math.sqrt(extent)).astype(jnp.bfloat16)

def analysis(image):
    below = jnp.concatenate([image[:, 1:], jnp.zeros_like(image[:, :1])], axis=1)
    right = jnp.concatenate([image[:, :, 1:], jnp.zeros_like(image[:, :, :1])], axis=2)
    return jnp.stack([below - image, right - image], axis=1) * ROOT_HALF

def synthesis(coeffs):
    vertical = coeffs[:, 0]
    horizontal = coeffs[:, 1]
    above = jnp.concatenate([jnp.zeros_like(vertical[:, :1]), vertical[:, :-1]], axis=1)
    leftward = jnp.concatenate([jnp.zeros_like(horizontal[:, :, :1]), horizontal[:, :, :-1]], axis=2)
    return (above - vertical + leftward - horizontal) * ROOT_HALF

def measure_one(operands, table):
    extrap_one, tiles_one, pattern_one, live_one = operands
    grid = jnp.dot(extrap_one.astype(jnp.bfloat16), table, preferred_element_type=jnp.float32)
    grid = lax.optimization_barrier(grid.astype(jnp.bfloat16))
    blocks = grid.reshape(H * KB, 2, BLK)
    picked = blocks[pattern_one]
    seen = jnp.einsum('bkrg,bkvg->brv', picked.astype(jnp.float32), tiles_one.astype(jnp.float32))
    return seen * live_one[:, None, None]

def adjoint_one(operands, table):
    dual_one, tiles_one, pattern_one, live_one = operands
    weights = lax.optimization_barrier(dual_one.astype(jnp.bfloat16)).astype(jnp.float32)
    contrib = jnp.einsum('brv,bkvg->bkrg', weights, tiles_one.astype(jnp.float32))
    contrib = contrib * live_one[:, None, None, None]
    grid_adj = jnp.zeros((H * KB, 2, BLK), jnp.float32).at[pattern_one.reshape(-1)].add(contrib.reshape(-1, 2, BLK))
    rounded = grid_adj.reshape(H, 2 * W).astype(jnp.bfloat16)
    return jnp.dot(rounded, table.T, preferred_element_type=jnp.float32)

def reference(x_init, u_init, v_init, observed, tiles, pattern, counts, facet_bounds):
    table = dft_table(W, BLK)
    live = (jnp.arange(VB, dtype=jnp.int32)[None, :] < counts[:, None]).astype(jnp.float32)
    row_ids = jnp.arange(H, dtype=jnp.int32)
    inside = (row_ids[None, :] >= facet_bounds[:, 0:1]) & (row_ids[None, :] < facet_bounds[:, 1:2])
    cover = lax.optimization_barrier(jnp.sum(inside.astype(jnp.float32), axis=0))
    radius = RADIUS / cover
    image, prior_dual, data_dual = (x_init, u_init, v_init)
    for rounds in range(ITERS):
        back = lax.map(lambda operands: adjoint_one(operands, table), (data_dual, tiles, pattern, live))
        image_next = jnp.maximum(image - STEP_PRIMAL * (synthesis(prior_dual) + back), 0.0)
        extrap = 2.0 * image_next - image
        pushed = prior_dual + STEP_PRIOR * analysis(extrap)
        norms = jnp.sqrt(lax.optimization_barrier(jnp.sum(pushed * pushed, axis=0)) + 1e-06)
        prior_dual = pushed * jnp.minimum(1.0, radius[None, None, :, None] / norms[None])
        seen = lax.map(lambda operands: measure_one(operands, table), (extrap, tiles, pattern, live))
        data_dual = (data_dual + STEP_DATA * (seen - observed)) * live[:, :, None, None] / (1.0 + STEP_DATA)
        image = image_next
    return (image, prior_dual, data_dual)
```

```python
import functools
import math

import jax
import jax.numpy as jnp
import ml_dtypes
import numpy as np
from jax import lax
from jax.experimental import pallas as pl
from jax.experimental.pallas import tpu as pltpu
from jax.sharding import PartitionSpec as P

ITERS = 2

STEP_PRIMAL = 0.5
STEP_PRIOR = 0.5
STEP_DATA = 1.0
RADIUS = 12.0
ROOT_HALF = 0.7071067811865476

GROUP = 8
RING = 32
CHUNK = 128
PIECE = 512


def shifted(shard, axis, by):
    count = lax.axis_size(axis)
    pairs = [(i, i + by) for i in range(count) if 0 <= i + by < count]
    return lax.ppermute(shard, axis, pairs)


def split_divide(value, by):
    if by & (by - 1) == 0:
        return lax.shift_right_logical(value, by.bit_length() - 1), value & (by - 1)
    return value // by, value % by


def transform_tables(extent, tile):
    j = np.arange(extent, dtype=np.int64)
    g = np.arange(tile, dtype=np.int64)
    angle = (g[:, None] * j[None, :] % extent) * (2.0 * math.pi / extent)
    cos, sin = np.cos(angle) / math.sqrt(extent), np.sin(angle) / math.sqrt(extent)
    adjoint = np.concatenate(
        [np.concatenate([cos, sin], 1), np.concatenate([-sin, cos], 1)], 0
    )
    forward = np.concatenate(
        [np.concatenate([cos.T, -sin.T], 1), np.concatenate([-sin.T, -cos.T], 1)], 0
    )
    high = forward.astype(ml_dtypes.bfloat16)
    low = (forward - high.astype(np.float64)).astype(ml_dtypes.bfloat16)
    blocks = extent // tile
    turn = (np.arange(blocks)[:, None] * np.arange(tile)[None, :] % blocks) * (2.0 * math.pi / blocks)
    return (
        adjoint.astype(ml_dtypes.bfloat16),
        high,
        low,
        np.cos(turn).astype(np.float32),
        np.sin(turn).astype(np.float32),
    )


def iteration_kernel(first, dims, *refs):
    chans, slots, blocks_per, rows, extent, tile = dims
    per_row = extent // tile
    cap = chans * slots * blocks_per
    refs = list(refs)
    ent, off = refs[:2]
    v_ref, tiles_ref, x_ref, u_ref, carry_ref = refs[2:7]
    refs = refs[7:]
    if not first:
        last_ref, tot_ref, rad_ref = refs[:3]
        refs = refs[3:]
    adj_ref, hi_ref, lo_ref, cos_ref, sin_ref = refs[:5]
    img_ref, push_ref, sum_ref, seen_ref, ef_ref, el_ref, pl_ref = refs[5:12]
    big, g_re, g_im, ph_c, ph_s, bacc, ebuf, tbuf, sems = refs[12:21]
    if not first:
        us, scale = refs[21:23]
    c = pl.program_id(0)
    total = off[chans]
    groups = lax.shift_right_logical(total + (GROUP - 1), GROUP.bit_length() - 1)
    chunks = lax.shift_right_logical(total + (CHUNK - 1), CHUNK.bit_length() - 1)

    def entry(q):
        where_it_goes, source = split_divide(ent[q], cap)
        row, block = split_divide(where_it_goes, per_row)
        return source, row, block

    def issue(group):
        slot = lax.rem(group, RING)
        for t in range(GROUP):
            source, _, _ = entry(group * GROUP + t)
            pltpu.make_async_copy(
                tiles_ref.at[source], tbuf.at[slot * GROUP + t], sems.at[slot]
            ).start()

    def await_group(group):
        slot = lax.rem(group, RING)
        pltpu.make_async_copy(
            tiles_ref.at[pl.ds(0, GROUP)], tbuf.at[pl.ds(slot * GROUP, GROUP)], sems.at[slot]
        ).wait()
        return slot * GROUP

    def prime():
        @pl.loop(0, jnp.minimum(groups, RING))
        def _(group):
            issue(group)

    def widen(value):
        return jnp.concatenate([value] * (PIECE // tile), axis=1)

    @pl.when(c == 0)
    def _():
        prime()
        sum_ref[...] = jnp.zeros_like(sum_ref)
        if not first:
            for band in range(2):
                for r in range(0, rows, 8):
                    norms = jnp.sqrt(tot_ref[band, r : r + 8] + 1e-06)
                    scale[band, r : r + 8] = jnp.minimum(1.0, rad_ref[r : r + 8] / norms)

        @pl.loop(0, groups)
        def _(group):
            base = await_group(group)
            re, im, co, si = [], [], [], []
            for t in range(GROUP):
                source, _, block = entry(group * GROUP + t)
                place, _ = split_divide(source, blocks_per)
                weights = v_ref[place].astype(jnp.bfloat16)
                contrib = jnp.dot(weights, tbuf[base + t], preferred_element_type=jnp.float32)
                re.append(contrib[0:1])
                im.append(contrib[1:2])
                co.append(cos_ref[pl.ds(block, 1), :])
                si.append(sin_ref[pl.ds(block, 1), :])
            at = pl.ds(pl.multiple_of(group * GROUP, GROUP), GROUP)
            g_re[at, :] = jnp.concatenate(re, axis=0)
            g_im[at, :] = jnp.concatenate(im, axis=0)
            ph_c[at, :] = jnp.concatenate(co, axis=0)
            ph_s[at, :] = jnp.concatenate(si, axis=0)

            @pl.when(group + RING < groups)
            def _():
                issue(group + RING)

        @pl.loop(0, chunks)
        def _(chunk):
            at = pl.ds(pl.multiple_of(chunk * CHUNK, CHUNK), CHUNK)
            lhs = jnp.concatenate([g_re[at, :], g_im[at, :]], axis=1).astype(jnp.bfloat16)
            turn_c, turn_s = widen(ph_c[at, :]), widen(ph_s[at, :])
            for j in range(0, extent, PIECE):
                even = jnp.dot(lhs, adj_ref[:, j : j + PIECE], preferred_element_type=jnp.float32)
                odd = jnp.dot(
                    lhs,
                    adj_ref[:, extent + j : extent + j + PIECE],
                    preferred_element_type=jnp.float32,
                )
                big[at, j : j + PIECE] = turn_c * even - turn_s * odd

        prime()

    start, end = off[c], off[c + 1]
    bacc[...] = jnp.zeros_like(bacc)

    @pl.loop(start, end)
    def _(q):
        _, row, _ = entry(q)
        bacc[pl.ds(row, 1), :] += big[pl.ds(q, 1), :]

    if not first:
        us[0, 7:8] = carry_ref[pl.ds(c, 1), :]
        for band in range(2):
            for r in range(0, rows, 8):
                value = u_ref[0, band, r : r + 8]
                if band == 0 and r == rows - 8:
                    value = jnp.concatenate([value[:7], last_ref[pl.ds(c, 1), :]], axis=0)
                us[band, r + 8 : r + 16] = value * scale[band, r : r + 8]

    def dual(band, r):
        return u_ref[0, band, r : r + 8] if first else us[band, r + 8 : r + 16]

    def dual_above(r):
        if not first:
            return us[0, r + 7 : r + 15]
        if r:
            return u_ref[0, 0, r - 1 : r + 7]
        return jnp.concatenate([carry_ref[pl.ds(c, 1), :], u_ref[0, 0, 0:7]], axis=0)

    column = lax.broadcasted_iota(jnp.int32, (8, extent), 1)
    for r in range(0, rows, 8):
        across = dual(1, r)
        leftward = jnp.where(column == 0, 0.0, pltpu.roll(across, 1, 1))
        synthesis = (dual_above(r) - dual(0, r) + leftward - across) * ROOT_HALF
        image = x_ref[0, r : r + 8]
        image_next = jnp.maximum(image - STEP_PRIMAL * (synthesis + bacc[r : r + 8]), 0.0)
        img_ref[0, r : r + 8] = image_next
        ebuf[r : r + 8] = 2.0 * image_next - image
    ebuf[rows : rows + 8] = jnp.zeros((8, extent), jnp.float32)

    @pl.loop(start, end)
    def _(q):
        _, row, _ = entry(q)
        big[pl.ds(q, 1), :] = ebuf[pl.ds(row, 1), :]

    for r in range(0, rows, 8):
        here = ebuf[r : r + 8]
        below = ebuf[r + 1 : r + 9]
        right = jnp.where(column == extent - 1, 0.0, pltpu.roll(here, extent - 1, 1))
        vertical = dual(0, r) + (STEP_PRIOR * ROOT_HALF) * (below - here)
        horizontal = dual(1, r) + (STEP_PRIOR * ROOT_HALF) * (right - here)
        push_ref[0, 0, r : r + 8] = vertical
        push_ref[0, 1, r : r + 8] = horizontal
        sum_ref[0, r : r + 8] += vertical * vertical
        sum_ref[1, r : r + 8] += horizontal * horizontal
        if r == rows - 8:
            pl_ref[pl.ds(c, 1), :] = vertical[7:8]
    ef_ref[pl.ds(c, 1), :] = ebuf[0:1]
    el_ref[pl.ds(c, 1), :] = ebuf[rows - 1 : rows]

    @pl.when(c == chans - 1)
    def _():
        seen_ref[...] = jnp.zeros_like(seen_ref)

        @pl.loop(0, chunks)
        def _(chunk):
            at = pl.ds(pl.multiple_of(chunk * CHUNK, CHUNK), CHUNK)
            turn_c, turn_s = widen(ph_c[at, :]), widen(ph_s[at, :])
            grid = jnp.zeros((CHUNK, 2 * tile), jnp.float32)
            for j in range(0, extent, PIECE):
                value = big[at, j : j + PIECE].astype(jnp.bfloat16).astype(jnp.float32)
                for turn, base in ((turn_c, j), (turn_s, extent + j)):
                    turned = value * turn
                    high = turned.astype(jnp.bfloat16)
                    low = (turned - high.astype(jnp.float32)).astype(jnp.bfloat16)
                    table = hi_ref[base : base + PIECE, :]
                    grid += jnp.dot(high, table, preferred_element_type=jnp.float32)
                    grid += jnp.dot(low, table, preferred_element_type=jnp.float32)
                    grid += jnp.dot(
                        high, lo_ref[base : base + PIECE, :], preferred_element_type=jnp.float32
                    )
            g_re[at, :] = grid[:, :tile]
            g_im[at, :] = grid[:, tile:]

        @pl.loop(0, groups)
        def _(group):
            base = await_group(group)
            at = pl.ds(pl.multiple_of(group * GROUP, GROUP), GROUP)
            lhs = jnp.concatenate([g_re[at, :], g_im[at, :]], axis=0).astype(jnp.bfloat16)
            for t in range(GROUP):
                q = group * GROUP + t
                source, _, _ = entry(q)
                place, _ = split_divide(source, blocks_per)
                part = lax.dot_general(
                    lhs, tbuf[base + t], (((1,), (1,)), ((), ())), preferred_element_type=jnp.float32
                )
                part = jnp.concatenate([part[t : t + 1], part[GROUP + t : GROUP + t + 1]], axis=0)
                seen_ref[place] += jnp.where(q < total, part, 0.0)

            @pl.when(group + RING < groups)
            def _():
                issue(group + RING)


def iteration(first, tables, ent, off, v, tiles, x, u, carry, extra=()):
    chans, rows, extent = x.shape
    tile = tiles.shape[-1]
    slots = v.shape[0] // chans
    blocks_per = tiles.shape[0] // v.shape[0]
    cap = ent.shape[0]
    dims = (chans, slots, blocks_per, rows, extent, tile)

    def whole(shape):
        return pl.BlockSpec(shape, lambda c, *_: (0,) * len(shape), pipeline_mode=pl.Buffered(1))

    def per_channel(shape):
        return pl.BlockSpec((1,) + shape, lambda c, *_: (c,) + (0,) * len(shape))

    image_spec, dual_spec = per_channel((rows, extent)), per_channel((2, rows, extent))
    resident = lambda shape: jax.ShapeDtypeStruct(shape, jnp.float32)
    outs = [x.shape, u.shape, (2, rows, extent), v.shape] + [(chans, extent)] * 3
    rows_cap = max(cap, CHUNK)
    scratch = [
        pltpu.VMEM((rows_cap, extent), jnp.float32),
        pltpu.VMEM((rows_cap, tile), jnp.float32),
        pltpu.VMEM((rows_cap, tile), jnp.float32),
        pltpu.VMEM((rows_cap, tile), jnp.float32),
        pltpu.VMEM((rows_cap, tile), jnp.float32),
        pltpu.VMEM((rows, extent), jnp.float32),
        pltpu.VMEM((rows + 8, extent), jnp.float32),
        pltpu.VMEM((RING * GROUP, tile, tile), jnp.bfloat16),
        pltpu.SemaphoreType.DMA((RING,)),
    ]
    if not first:
        scratch += [
            pltpu.VMEM((2, rows + 8, extent), jnp.float32),
            pltpu.VMEM((2, rows, extent), jnp.float32),
        ]
    operands = [v, tiles, x, u, carry, *extra, *tables]
    in_specs = [whole(v.shape), pl.BlockSpec(memory_space=pl.ANY), image_spec, dual_spec]
    in_specs += [whole(a.shape) for a in operands[4:]]
    return pl.pallas_call(
        functools.partial(iteration_kernel, first, dims),
        out_shape=[resident(s) for s in outs],
        grid_spec=pltpu.PrefetchScalarGridSpec(
            num_scalar_prefetch=2,
            grid=(chans,),
            in_specs=in_specs,
            out_specs=[image_spec, dual_spec] + [whole(s) for s in outs[2:]],
            scratch_shapes=scratch,
        ),
        compiler_params=pltpu.CompilerParams(
            dimension_semantics=("arbitrary",), vmem_limit_bytes=58 << 20
        ),
        name="primal_dual_first" if first else "primal_dual_next",
    )(ent, off, *operands)


def shrink_kernel(push_ref, last_ref, tot_ref, rad_ref, out_ref, scale):
    rows = push_ref.shape[2]
    c = pl.program_id(0)

    @pl.when(c == 0)
    def _():
        for band in range(2):
            for r in range(0, rows, 8):
                norms = jnp.sqrt(tot_ref[band, r : r + 8] + 1e-06)
                scale[band, r : r + 8] = jnp.minimum(1.0, rad_ref[r : r + 8] / norms)

    for band in range(2):
        for r in range(0, rows, 8):
            value = push_ref[0, band, r : r + 8]
            if band == 0 and r == rows - 8:
                value = jnp.concatenate([value[:7], last_ref[pl.ds(c, 1), :]], axis=0)
            out_ref[0, band, r : r + 8] = value * scale[band, r : r + 8]


def shrink(push, last, total, radius):
    chans, _, rows, extent = push.shape

    def whole(shape):
        return pl.BlockSpec(shape, lambda c: (0,) * len(shape), pipeline_mode=pl.Buffered(1))

    dual_spec = pl.BlockSpec((1, 2, rows, extent), lambda c: (c, 0, 0, 0))
    return pl.pallas_call(
        shrink_kernel,
        out_shape=jax.ShapeDtypeStruct(push.shape, jnp.float32),
        grid=(chans,),
        in_specs=[dual_spec, whole(last.shape), whole(total.shape), whole(radius.shape)],
        out_specs=dual_spec,
        scratch_shapes=[pltpu.VMEM((2, rows, extent), jnp.float32)],
        compiler_params=pltpu.CompilerParams(
            dimension_semantics=("arbitrary",), vmem_limit_bytes=32 << 20
        ),
        name="shrink",
    )(push, last, total, radius)


def exchange(value, axis, bit):
    count = lax.axis_size(axis)
    return lax.ppermute(value, axis, [(i, i ^ bit) for i in range(count)])


def halve(value, axis, bits):
    index = lax.axis_index(axis)
    for bit in bits:
        half = value.shape[0] // 2
        mine = (index // bit) % 2
        keep = lax.dynamic_slice_in_dim(value, mine * half, half, 0)
        send = lax.dynamic_slice_in_dim(value, (1 - mine) * half, half, 0)
        value = keep + exchange(send, axis, bit)
    return value


def double(value, axis, bits):
    index = lax.axis_index(axis)
    for bit in reversed(bits):
        other = exchange(value, axis, bit)
        first = (index // bit) % 2 == 0
        value = jnp.concatenate(
            [jnp.where(first, value, other), jnp.where(first, other, value)], axis=0
        )
    return value


def shard_of(value, axis, bits):
    index = lax.axis_index(axis)
    for bit in bits:
        half = value.shape[0] // 2
        value = lax.dynamic_slice_in_dim(value, ((index // bit) % 2) * half, half, 0)
    return value


def chan_orders(count):
    bits = [1 << k for k in range(count.bit_length() - 1)]
    inner, outer = bits[:1], bits[1:]
    half = len(outer) // 2
    return inner + outer[:half] + outer[half:], inner + outer[half:] + outer[:half]


def sum_over_channels(local_sum):
    count = lax.axis_size("chan")
    if count & (count - 1) or local_sum.shape[1] % count:
        return lax.psum(local_sum, "chan")
    order_a, order_b = chan_orders(count)
    vertical, horizontal = local_sum[0], local_sum[1]
    vertical = double(halve(vertical, "chan", order_a), "chan", order_a)
    horizontal = double(halve(horizontal, "chan", order_b), "chan", order_b)
    return jnp.stack([vertical, horizontal])


def update_data(seen, data_dual, observed, live):
    count = lax.axis_size("facet")
    if count & (count - 1) or seen.shape[0] % count:
        seen = lax.psum(seen, "facet")
        return (data_dual + STEP_DATA * (seen - observed)) * live / (1.0 + STEP_DATA)
    bits = [1 << k for k in range(count.bit_length() - 1)]
    seen = halve(seen, "facet", bits)
    data_dual, observed, live = (shard_of(a, "facet", bits) for a in (data_dual, observed, live))
    fresh = (data_dual + STEP_DATA * (seen - observed)) * live / (1.0 + STEP_DATA)
    return double(fresh, "facet", bits)


def local(x_init, u_init, v_init, observed, tiles, pattern, counts, facet_bounds):
    chans, rows, extent = x_init.shape
    slots, blocks_per = pattern.shape[1:]
    tile = tiles.shape[-1]
    per_row = extent // tile
    facet = lax.axis_index("facet")
    row_start = facet * rows
    cap = chans * slots * blocks_per
    tables = [jnp.asarray(t) for t in transform_tables(extent, tile)]

    live = jnp.arange(slots, dtype=jnp.int32)[None, :] < counts[:, None]
    local_index = pattern - row_start * per_row
    keep = (local_index >= 0) & (local_index < rows * per_row) & live[:, :, None]
    keep = keep.reshape(cap)
    order = jnp.arange(cap, dtype=jnp.int32)
    ahead = jnp.sum(
        (keep[None, :] & (order[None, :] < order[:, None])).astype(jnp.int32), axis=1
    )
    packed = jnp.where(keep, local_index.reshape(cap) * cap + order, 0)
    ent = jnp.sum(
        jnp.where(keep[None, :] & (ahead[None, :] == order[:, None]), packed[None, :], 0), axis=1
    )
    kept = jnp.sum(keep.reshape(chans, -1).astype(jnp.int32), axis=1)
    edges = jnp.arange(chans + 1, dtype=jnp.int32)
    off = jnp.sum(jnp.where(edges[None, :chans] < edges[:, None], kept[None, :], 0), axis=1)

    row_ids = row_start - 1 + jnp.arange(rows + 1, dtype=jnp.int32)
    inside = (row_ids[None, :] >= facet_bounds[:, 0:1]) & (row_ids[None, :] < facet_bounds[:, 1:2])
    cover = jnp.sum(inside.astype(jnp.float32), axis=0)
    radius = (RADIUS / cover)[:, None]
    radius, radius_above = radius[1:], radius[0]

    live_float = jnp.broadcast_to(live.reshape(-1, 1, 1).astype(jnp.float32), (chans * slots, 1, 1))
    observed = observed.reshape(chans * slots, 2, tile)
    data_dual = v_init.reshape(chans * slots, 2, tile)
    tiles = tiles.reshape(cap, tile, tile)
    image, dual = x_init, u_init
    carry = shifted(u_init[:, 0, -1, :], "facet", 1)
    extra = ()
    for rounds in range(ITERS):
        image, dual, local_sum, seen, first_row, last_row, pushed_last = iteration(
            rounds == 0, tables, ent, off, data_dual, tiles, image, dual, carry, extra
        )
        half_step = STEP_PRIOR * ROOT_HALF
        pushed_last = pushed_last + half_step * shifted(first_row, "facet", -1)
        local_sum = lax.dynamic_update_slice(
            local_sum, jnp.sum(pushed_last * pushed_last, axis=0)[None, None], (0, rows - 1, 0)
        )
        total = sum_over_channels(local_sum)
        data_dual = update_data(seen, data_dual, observed, live_float)
        extra = (pushed_last, total, radius)
        if rounds + 1 < ITERS:
            above = carry + half_step * (first_row - shifted(last_row, "facet", 1))
            norms = jnp.sqrt(shifted(total[0, rows - 1 :], "facet", 1) + 1e-06)
            carry = jnp.where(facet > 0, above * jnp.minimum(1.0, radius_above / norms), 0.0)
    return (
        image,
        shrink(dual, *extra),
        data_dual.reshape(v_init.shape),
    )


def solution(mesh):
    in_specs = (
        P("chan", "facet", None),
        P("chan", None, "facet", None),
        P("chan", None, None, None),
        P("chan", None, None, None),
        P("chan", None, None, None, None),
        P("chan", None, None),
        P("chan"),
        P(),
    )
    out_specs = (
        P("chan", "facet", None),
        P("chan", None, "facet", None),
        P("chan", None, None, None),
    )
    return jax.shard_map(local, mesh=mesh, in_specs=in_specs, out_specs=out_specs, check_vma=False)
```

```python
import functools
import math

import jax
import jax.numpy as jnp
import ml_dtypes
import numpy as np
from jax import lax
from jax.experimental import pallas as pl
from jax.experimental.pallas import tpu as pltpu
from jax.sharding import PartitionSpec as P

ITERS = 2

STEP_PRIMAL = 0.5
STEP_PRIOR = 0.5
STEP_DATA = 1.0
RADIUS = 12.0
ROOT_HALF = 0.7071067811865476

GROUP = 8
RING = 8
CHUNK = 320
PIECE = 512
DEPTH = 4


def shifted(shard, axis, by):
    count = lax.axis_size(axis)
    pairs = [(i, i + by) for i in range(count) if 0 <= i + by < count]
    return lax.ppermute(shard, axis, pairs)


def split_divide(value, by):
    if by & (by - 1) == 0:
        return lax.shift_right_logical(value, by.bit_length() - 1), value & (by - 1)
    return value // by, value % by


def transform_tables(extent, tile):
    j = np.arange(extent, dtype=np.int64)
    g = np.arange(tile, dtype=np.int64)
    angle = (g[:, None] * j[None, :] % extent) * (2.0 * math.pi / extent)
    cos, sin = np.cos(angle) / math.sqrt(extent), np.sin(angle) / math.sqrt(extent)
    adjoint = np.concatenate(
        [np.concatenate([cos, sin], 1), np.concatenate([-sin, cos], 1)], 0
    )
    forward = np.concatenate(
        [np.concatenate([cos.T, -sin.T], 1), np.concatenate([-sin.T, -cos.T], 1)], 0
    )
    high = forward.astype(ml_dtypes.bfloat16)
    low = (forward - high.astype(np.float64)).astype(ml_dtypes.bfloat16)
    blocks = extent // tile
    turn = (np.arange(blocks)[:, None] * np.arange(tile)[None, :] % blocks) * (2.0 * math.pi / blocks)
    return (
        adjoint.astype(ml_dtypes.bfloat16),
        high,
        low,
        np.cos(turn).astype(np.float32),
        np.sin(turn).astype(np.float32),
    )


def iteration_kernel(first, dims, *refs):
    chans, slots, blocks_per, rows, extent, tile = dims
    per_row = extent // tile
    cap = chans * slots * blocks_per
    refs = list(refs)
    ent, off = refs[:2]
    v_ref, tiles_ref, x_hbm, u_hbm, carry_ref = refs[2:7]
    refs = refs[7:]
    if not first:
        last_ref, tot_ref, rad_ref = refs[:3]
        refs = refs[3:]
    tables, (cos_ref, sin_ref) = refs[:3], refs[3:5]
    img_hbm, push_hbm, sum_ref, seen_ref, ef_ref, el_ref, pl_ref = refs[5:12]
    big, g_re, g_im, ph_c, ph_s, bacc, ebuf, tbuf, sems = refs[12:21]
    adj_ref, hi_ref, lo_ref, table_sems = refs[21:25]
    x_in, u_in, x_out, u_out, in_sems, out_sems = refs[25:31]
    if not first:
        us, scale = refs[31:33]
    c = pl.program_id(0)
    total = off[chans]
    groups = lax.shift_right_logical(total + (GROUP - 1), GROUP.bit_length() - 1)
    chunks = sum(
        (total > begin).astype(jnp.int32) for begin in range(0, cap, CHUNK)
    )
    slot = lax.rem(c, DEPTH)
    x_ref, u_ref = x_in.at[pl.ds(slot, 1)], u_in.at[pl.ds(slot, 1)]
    img_ref, push_ref = x_out.at[pl.ds(slot, 1)], u_out.at[pl.ds(slot, 1)]

    def entry(q):
        where_it_goes, source = split_divide(ent[q], cap)
        row, block = split_divide(where_it_goes, per_row)
        return source, row, block

    def issue(group):
        slot = lax.rem(group, RING)
        for t in range(GROUP):
            source, _, _ = entry(group * GROUP + t)
            pltpu.make_async_copy(
                tiles_ref.at[source], tbuf.at[slot * GROUP + t], sems.at[slot]
            ).start()

    def await_group(group):
        slot = lax.rem(group, RING)
        pltpu.make_async_copy(
            tiles_ref.at[pl.ds(0, GROUP)], tbuf.at[pl.ds(slot * GROUP, GROUP)], sems.at[slot]
        ).wait()
        return slot * GROUP

    def prime():
        @pl.loop(0, jnp.minimum(groups, RING))
        def _(group):
            issue(group)

    def copies_in(channel):
        place = lax.rem(channel, DEPTH)
        return (
            pltpu.make_async_copy(x_hbm.at[channel], x_in.at[place], in_sems.at[0, place]),
            pltpu.make_async_copy(u_hbm.at[channel], u_in.at[place], in_sems.at[1, place]),
        )

    def copies_out(channel):
        place = lax.rem(channel, DEPTH)
        return (
            pltpu.make_async_copy(x_out.at[place], img_hbm.at[channel], out_sems.at[0, place]),
            pltpu.make_async_copy(u_out.at[place], push_hbm.at[channel], out_sems.at[1, place]),
        )

    def table_copy(k):
        return pltpu.make_async_copy(tables[k], (adj_ref, hi_ref, lo_ref)[k], table_sems.at[k])

    def widen(value):
        return jnp.concatenate([value] * (PIECE // tile), axis=1)

    @pl.when(c == 0)
    def _():
        prime()
        for k in range(3):
            table_copy(k).start()
        for channel in range(min(DEPTH, chans)):
            for copy in copies_in(jnp.int32(channel)):
                copy.start()
        sum_ref[...] = jnp.zeros_like(sum_ref)
        if not first:
            for band in range(2):
                for r in range(0, rows, 8):
                    norms = jnp.sqrt(tot_ref[band, r : r + 8] + 1e-06)
                    scale[band, r : r + 8] = jnp.minimum(1.0, rad_ref[r : r + 8] / norms)

        @pl.loop(0, groups)
        def _(group):
            base = await_group(group)
            re, im, co, si = [], [], [], []
            for t in range(GROUP):
                source, _, block = entry(group * GROUP + t)
                place, _ = split_divide(source, blocks_per)
                weights = v_ref[place].astype(jnp.bfloat16)
                contrib = jnp.dot(weights, tbuf[base + t], preferred_element_type=jnp.float32)
                re.append(contrib[0:1])
                im.append(contrib[1:2])
                co.append(cos_ref[pl.ds(block, 1), :])
                si.append(sin_ref[pl.ds(block, 1), :])
            at = pl.ds(pl.multiple_of(group * GROUP, GROUP), GROUP)
            g_re[at, :] = jnp.concatenate(re, axis=0)
            g_im[at, :] = jnp.concatenate(im, axis=0)
            ph_c[at, :] = jnp.concatenate(co, axis=0)
            ph_s[at, :] = jnp.concatenate(si, axis=0)

            @pl.when(group + RING < groups)
            def _():
                issue(group + RING)

        table_copy(0).wait()

        @pl.loop(0, chunks)
        def _(chunk):
            at = pl.ds(pl.multiple_of(chunk * CHUNK, CHUNK), CHUNK)
            lhs = jnp.concatenate([g_re[at, :], g_im[at, :]], axis=1).astype(jnp.bfloat16)
            turn_c, turn_s = widen(ph_c[at, :]), widen(ph_s[at, :])
            for j in range(0, extent, PIECE):
                even = jnp.dot(lhs, adj_ref[:, j : j + PIECE], preferred_element_type=jnp.float32)
                odd = jnp.dot(
                    lhs,
                    adj_ref[:, extent + j : extent + j + PIECE],
                    preferred_element_type=jnp.float32,
                )
                big[at, j : j + PIECE] = turn_c * even - turn_s * odd

        prime()

    start, end = off[c], off[c + 1]
    bacc[...] = jnp.zeros_like(bacc)

    @pl.loop(start, end)
    def _(q):
        _, row, _ = entry(q)
        bacc[pl.ds(row, 1), :] += big[pl.ds(q, 1), :]

    for copy in copies_in(c):
        copy.wait()

    @pl.when(c >= DEPTH)
    def _():
        for copy in copies_out(c - DEPTH):
            copy.wait()

    if not first:
        us[0, 7:8] = carry_ref[pl.ds(c, 1), :]
        for band in range(2):
            for r in range(0, rows, 8):
                value = u_ref[0, band, r : r + 8]
                if band == 0 and r == rows - 8:
                    value = jnp.concatenate([value[:7], last_ref[pl.ds(c, 1), :]], axis=0)
                us[band, r + 8 : r + 16] = value * scale[band, r : r + 8]

    def dual(band, r):
        return u_ref[0, band, r : r + 8] if first else us[band, r + 8 : r + 16]

    def dual_above(r):
        if not first:
            return us[0, r + 7 : r + 15]
        if r:
            return u_ref[0, 0, r - 1 : r + 7]
        return jnp.concatenate([carry_ref[pl.ds(c, 1), :], u_ref[0, 0, 0:7]], axis=0)

    column = lax.broadcasted_iota(jnp.int32, (8, extent), 1)
    for r in range(0, rows, 8):
        across = dual(1, r)
        leftward = jnp.where(column == 0, 0.0, pltpu.roll(across, 1, 1))
        synthesis = (dual_above(r) - dual(0, r) + leftward - across) * ROOT_HALF
        image = x_ref[0, r : r + 8]
        image_next = jnp.maximum(image - STEP_PRIMAL * (synthesis + bacc[r : r + 8]), 0.0)
        img_ref[0, r : r + 8] = image_next
        ebuf[r : r + 8] = 2.0 * image_next - image
    ebuf[rows : rows + 8] = jnp.zeros((8, extent), jnp.float32)

    @pl.loop(start, end)
    def _(q):
        _, row, _ = entry(q)
        big[pl.ds(q, 1), :] = ebuf[pl.ds(row, 1), :]

    for r in range(0, rows, 8):
        here = ebuf[r : r + 8]
        below = ebuf[r + 1 : r + 9]
        right = jnp.where(column == extent - 1, 0.0, pltpu.roll(here, extent - 1, 1))
        vertical = dual(0, r) + (STEP_PRIOR * ROOT_HALF) * (below - here)
        horizontal = dual(1, r) + (STEP_PRIOR * ROOT_HALF) * (right - here)
        push_ref[0, 0, r : r + 8] = vertical
        push_ref[0, 1, r : r + 8] = horizontal
        sum_ref[0, r : r + 8] += vertical * vertical
        sum_ref[1, r : r + 8] += horizontal * horizontal
        if r == rows - 8:
            pl_ref[pl.ds(c, 1), :] = vertical[7:8]
    for copy in copies_out(c):
        copy.start()

    @pl.when(c + DEPTH < chans)
    def _():
        for copy in copies_in(c + DEPTH):
            copy.start()

    ef_ref[pl.ds(c, 1), :] = ebuf[0:1]
    el_ref[pl.ds(c, 1), :] = ebuf[rows - 1 : rows]

    @pl.when(c == chans - 1)
    def _():
        seen_ref[...] = jnp.zeros_like(seen_ref)
        table_copy(1).wait()
        table_copy(2).wait()

        @pl.loop(0, chunks)
        def _(chunk):
            at = pl.ds(pl.multiple_of(chunk * CHUNK, CHUNK), CHUNK)
            turn_c, turn_s = widen(ph_c[at, :]), widen(ph_s[at, :])
            grid = jnp.zeros((CHUNK, 2 * tile), jnp.float32)
            for j in range(0, extent, PIECE):
                value = big[at, j : j + PIECE].astype(jnp.bfloat16).astype(jnp.float32)
                for turn, base in ((turn_c, j), (turn_s, extent + j)):
                    turned = value * turn
                    high = turned.astype(jnp.bfloat16)
                    low = (turned - high.astype(jnp.float32)).astype(jnp.bfloat16)
                    table = hi_ref[base : base + PIECE, :]
                    grid += jnp.dot(high, table, preferred_element_type=jnp.float32)
                    grid += jnp.dot(low, table, preferred_element_type=jnp.float32)
                    grid += jnp.dot(
                        high, lo_ref[base : base + PIECE, :], preferred_element_type=jnp.float32
                    )
            g_re[at, :] = grid[:, :tile]
            g_im[at, :] = grid[:, tile:]

        @pl.loop(0, groups)
        def _(group):
            base = await_group(group)
            at = pl.ds(pl.multiple_of(group * GROUP, GROUP), GROUP)
            lhs = jnp.concatenate([g_re[at, :], g_im[at, :]], axis=0).astype(jnp.bfloat16)
            for t in range(GROUP):
                q = group * GROUP + t
                source, _, _ = entry(q)
                place, _ = split_divide(source, blocks_per)
                part = lax.dot_general(
                    lhs, tbuf[base + t], (((1,), (1,)), ((), ())), preferred_element_type=jnp.float32
                )
                part = jnp.concatenate([part[t : t + 1], part[GROUP + t : GROUP + t + 1]], axis=0)
                seen_ref[place] += jnp.where(q < total, part, 0.0)

            @pl.when(group + RING < groups)
            def _():
                issue(group + RING)

        for channel in range(max(chans - DEPTH, 0), chans):
            for copy in copies_out(jnp.int32(channel)):
                copy.wait()


def iteration(first, tables, ent, off, v, tiles, x, u, carry, extra=()):
    chans, rows, extent = x.shape
    tile = tiles.shape[-1]
    slots = v.shape[0] // chans
    blocks_per = tiles.shape[0] // v.shape[0]
    cap = ent.shape[0]
    dims = (chans, slots, blocks_per, rows, extent, tile)

    def whole(shape):
        return pl.BlockSpec(shape, lambda c, *_: (0,) * len(shape), pipeline_mode=pl.Buffered(1))

    outs = [x.shape, u.shape, (2, rows, extent), v.shape] + [(chans, extent)] * 3
    rows_cap = pl.cdiv(cap, CHUNK) * CHUNK
    scratch = [
        pltpu.VMEM((rows_cap, extent), jnp.float32),
        pltpu.VMEM((rows_cap, tile), jnp.float32),
        pltpu.VMEM((rows_cap, tile), jnp.float32),
        pltpu.VMEM((rows_cap, tile), jnp.float32),
        pltpu.VMEM((rows_cap, tile), jnp.float32),
        pltpu.VMEM((rows, extent), jnp.float32),
        pltpu.VMEM((rows + 8, extent), jnp.float32),
        pltpu.VMEM((RING * GROUP, tile, tile), jnp.bfloat16),
        pltpu.SemaphoreType.DMA((RING,)),
        *(pltpu.VMEM(t.shape, t.dtype) for t in tables[:3]),
        pltpu.SemaphoreType.DMA((3,)),
        *[pltpu.VMEM((DEPTH, rows, extent), jnp.float32), pltpu.VMEM((DEPTH, 2, rows, extent), jnp.float32)] * 2,
        *[pltpu.SemaphoreType.DMA((2, DEPTH))] * 2,
    ]
    if not first:
        scratch += [
            pltpu.VMEM((2, rows + 8, extent), jnp.float32),
            pltpu.VMEM((2, rows, extent), jnp.float32),
        ]
    pin = lambda a: pltpu.with_memory_space_constraint(a, pltpu.HBM)
    x, u, tiles = pin(x), pin(u), pin(tiles)
    v = pin(v) if first else v
    tables = [pin(t) for t in tables]
    in_hbm = pl.BlockSpec(memory_space=pltpu.HBM)
    operands = [v, tiles, x, u, carry, *extra, *tables]
    in_specs = [whole(v.shape), in_hbm, in_hbm, in_hbm]
    in_specs += [whole(a.shape) for a in (carry, *extra)] + [in_hbm] * 3
    in_specs += [whole(a.shape) for a in tables[3:]]
    return pl.pallas_call(
        functools.partial(iteration_kernel, first, dims),
        out_shape=[
            pltpu.HBM(s, jnp.float32) if k < 2 else jax.ShapeDtypeStruct(s, jnp.float32)
            for k, s in enumerate(outs)
        ],
        grid_spec=pltpu.PrefetchScalarGridSpec(
            num_scalar_prefetch=2,
            grid=(chans,),
            in_specs=in_specs,
            out_specs=[in_hbm] * 2 + [pl.BlockSpec(s, lambda c, *_, n=len(s): (0,) * n) for s in outs[2:]],
            scratch_shapes=scratch,
        ),
        compiler_params=pltpu.CompilerParams(
            dimension_semantics=("arbitrary",), vmem_limit_bytes=45 << 20
        ),
        name="primal_dual_first" if first else "primal_dual_next",
    )(ent, off, *operands)


def shrink_kernel(push_ref, last_ref, tot_ref, rad_ref, out_ref, scale):
    rows = push_ref.shape[2]
    c = pl.program_id(0)

    @pl.when(c == 0)
    def _():
        for band in range(2):
            for r in range(0, rows, 8):
                norms = jnp.sqrt(tot_ref[band, r : r + 8] + 1e-06)
                scale[band, r : r + 8] = jnp.minimum(1.0, rad_ref[r : r + 8] / norms)

    for band in range(2):
        for r in range(0, rows, 8):
            value = push_ref[0, band, r : r + 8]
            if band == 0 and r == rows - 8:
                value = jnp.concatenate([value[:7], last_ref[pl.ds(c, 1), :]], axis=0)
            out_ref[0, band, r : r + 8] = value * scale[band, r : r + 8]


def shrink(push, last, total, radius):
    chans, _, rows, extent = push.shape

    def whole(shape):
        return pl.BlockSpec(shape, lambda c: (0,) * len(shape), pipeline_mode=pl.Buffered(1))

    dual_spec = pl.BlockSpec((1, 2, rows, extent), lambda c: (c, 0, 0, 0))
    return pl.pallas_call(
        shrink_kernel,
        out_shape=jax.ShapeDtypeStruct(push.shape, jnp.float32),
        grid=(chans,),
        in_specs=[dual_spec, whole(last.shape), whole(total.shape), whole(radius.shape)],
        out_specs=dual_spec,
        scratch_shapes=[pltpu.VMEM((2, rows, extent), jnp.float32)],
        compiler_params=pltpu.CompilerParams(
            dimension_semantics=("arbitrary",), vmem_limit_bytes=8 << 20
        ),
        name="shrink",
    )(push, last, total, radius)


def exchange(value, axis, bit):
    count = lax.axis_size(axis)
    return lax.ppermute(value, axis, [(i, i ^ bit) for i in range(count)])


def halve(value, axis, bits):
    index = lax.axis_index(axis)
    for bit in bits:
        half = value.shape[0] // 2
        mine = (index // bit) % 2
        keep = lax.dynamic_slice_in_dim(value, mine * half, half, 0)
        send = lax.dynamic_slice_in_dim(value, (1 - mine) * half, half, 0)
        value = keep + exchange(send, axis, bit)
    return value


def double(value, axis, bits):
    index = lax.axis_index(axis)
    for bit in reversed(bits):
        other = exchange(value, axis, bit)
        first = (index // bit) % 2 == 0
        value = jnp.concatenate(
            [jnp.where(first, value, other), jnp.where(first, other, value)], axis=0
        )
    return value


def shard_of(value, axis, bits):
    index = lax.axis_index(axis)
    for bit in bits:
        half = value.shape[0] // 2
        value = lax.dynamic_slice_in_dim(value, ((index // bit) % 2) * half, half, 0)
    return value


def sum_over_channels(local_sum):
    count = lax.axis_size("chan")
    bands, rows, extent = local_sum.shape
    if count & (count - 1) or count < 2 or (bands * rows) % count:
        return lax.psum(local_sum, "chan")
    chips = count // 2
    index = lax.axis_index("chan") // 2
    value = halve(local_sum.reshape(bands * rows, extent), "chan", [1])
    value = value.reshape(chips, -1, extent)
    take = lambda at: lax.dynamic_index_in_dim(value, at, 0, False)
    parts = [exchange(take(index ^ d), "chan", 2 * d) for d in range(1, chips)]
    total = sum(parts, take(index))
    sums = [total] + [exchange(total, "chan", 2 * d) for d in range(1, chips)]
    placed = []
    for place in range(chips):
        chosen = sums[0]
        for d in range(1, chips):
            chosen = jnp.where((index ^ place) == d, sums[d], chosen)
        placed.append(chosen)
    value = double(jnp.concatenate(placed, axis=0), "chan", [1])
    return value.reshape(bands, rows, extent)


def update_data(seen, data_dual, observed, live):
    count = lax.axis_size("facet")
    if count & (count - 1) or seen.shape[0] % count:
        seen = lax.psum(seen, "facet")
        return (data_dual + STEP_DATA * (seen - observed)) * live / (1.0 + STEP_DATA)
    bits = [1 << k for k in range(count.bit_length() - 1)]
    seen = halve(seen, "facet", bits)
    data_dual, observed, live = (shard_of(a, "facet", bits) for a in (data_dual, observed, live))
    fresh = (data_dual + STEP_DATA * (seen - observed)) * live / (1.0 + STEP_DATA)
    return double(fresh, "facet", bits)


def local(x_init, u_init, v_init, observed, tiles, pattern, counts, facet_bounds):
    chans, rows, extent = x_init.shape
    slots, blocks_per = pattern.shape[1:]
    tile = tiles.shape[-1]
    per_row = extent // tile
    facet = lax.axis_index("facet")
    row_start = facet * rows
    cap = chans * slots * blocks_per
    tables = [jnp.asarray(t) for t in transform_tables(extent, tile)]

    live = jnp.arange(slots, dtype=jnp.int32)[None, :] < counts[:, None]
    local_index = pattern - row_start * per_row
    keep = (local_index >= 0) & (local_index < rows * per_row) & live[:, :, None]
    keep = keep.reshape(cap)
    order = jnp.arange(cap, dtype=jnp.int32)
    ahead = jnp.sum(
        (keep[None, :] & (order[None, :] < order[:, None])).astype(jnp.int32), axis=1
    )
    packed = jnp.where(keep, local_index.reshape(cap) * cap + order, 0)
    ent = jnp.sum(
        jnp.where(keep[None, :] & (ahead[None, :] == order[:, None]), packed[None, :], 0), axis=1
    )
    kept = jnp.sum(keep.reshape(chans, -1).astype(jnp.int32), axis=1)
    edges = jnp.arange(chans + 1, dtype=jnp.int32)
    off = jnp.sum(jnp.where(edges[None, :chans] < edges[:, None], kept[None, :], 0), axis=1)

    row_ids = row_start - 1 + jnp.arange(rows + 1, dtype=jnp.int32)
    inside = (row_ids[None, :] >= facet_bounds[:, 0:1]) & (row_ids[None, :] < facet_bounds[:, 1:2])
    cover = jnp.sum(inside.astype(jnp.float32), axis=0)
    radius = (RADIUS / cover)[:, None]
    radius, radius_above = radius[1:], radius[0]

    live_float = jnp.broadcast_to(live.reshape(-1, 1, 1).astype(jnp.float32), (chans * slots, 1, 1))
    observed = observed.reshape(chans * slots, 2, tile)
    data_dual = v_init.reshape(chans * slots, 2, tile)
    tiles = tiles.reshape(cap, tile, tile)
    image, dual = x_init, u_init
    carry = shifted(u_init[:, 0, -1, :], "facet", 1)
    extra = ()
    for rounds in range(ITERS):
        image, dual, local_sum, seen, first_row, last_row, pushed_last = iteration(
            rounds == 0, tables, ent, off, data_dual, tiles, image, dual, carry, extra
        )
        half_step = STEP_PRIOR * ROOT_HALF
        pushed_last = pushed_last + half_step * shifted(first_row, "facet", -1)
        local_sum = lax.dynamic_update_slice(
            local_sum, jnp.sum(pushed_last * pushed_last, axis=0)[None, None], (0, rows - 1, 0)
        )
        total = sum_over_channels(local_sum)
        data_dual = update_data(seen, data_dual, observed, live_float)
        extra = (pushed_last, total, radius)
        if rounds + 1 < ITERS:
            above = carry + half_step * (first_row - shifted(last_row, "facet", 1))
            norms = jnp.sqrt(shifted(total[0, rows - 1 :], "facet", 1) + 1e-06)
            carry = jnp.where(facet > 0, above * jnp.minimum(1.0, radius_above / norms), 0.0)
    return (
        image,
        shrink(dual, *extra),
        data_dual.reshape(v_init.shape),
    )


def solution(mesh):
    in_specs = (
        P("chan", "facet", None),
        P("chan", None, "facet", None),
        P("chan", None, None, None),
        P("chan", None, None, None),
        P("chan", None, None, None, None),
        P("chan", None, None),
        P("chan"),
        P(),
    )
    out_specs = (
        P("chan", "facet", None),
        P("chan", None, "facet", None),
        P("chan", None, None, None),
    )
    return jax.shard_map(local, mesh=mesh, in_specs=in_specs, out_specs=out_specs, check_vma=False)
```

```python
import functools
import math

import jax
import jax.numpy as jnp
import ml_dtypes
import numpy as np
from jax import lax
from jax.experimental import pallas as pl
from jax.experimental.pallas import tpu as pltpu
from jax.sharding import PartitionSpec as P

ITERS = 2

STEP_PRIMAL = 0.5
STEP_PRIOR = 0.5
STEP_DATA = 1.0
RADIUS = 12.0
ROOT_HALF = 0.7071067811865476

GROUP = 8
RING = 36
CHUNK = 352
PIECE = 512
DEPTH = 3


def shifted(shard, axis, by):
    count = lax.axis_size(axis)
    pairs = [(i, i + by) for i in range(count) if 0 <= i + by < count]
    return lax.ppermute(shard, axis, pairs)


def split_divide(value, by):
    if by & (by - 1) == 0:
        return lax.shift_right_logical(value, by.bit_length() - 1), value & (by - 1)
    return value // by, value % by


def transform_tables(extent, tile):
    j = np.arange(extent, dtype=np.int64)
    g = np.arange(tile, dtype=np.int64)
    angle = (g[:, None] * j[None, :] % extent) * (2.0 * math.pi / extent)
    cos, sin = np.cos(angle) / math.sqrt(extent), np.sin(angle) / math.sqrt(extent)
    adjoint = np.concatenate(
        [np.concatenate([cos, sin], 1), np.concatenate([-sin, cos], 1)], 0
    )
    forward = np.concatenate(
        [np.concatenate([cos.T, -sin.T], 1), np.concatenate([-sin.T, -cos.T], 1)], 0
    )
    high = forward.astype(ml_dtypes.bfloat16)
    low = (forward - high.astype(np.float64)).astype(ml_dtypes.bfloat16)
    blocks = extent // tile
    turn = (np.arange(blocks)[:, None] * np.arange(tile)[None, :] % blocks) * (2.0 * math.pi / blocks)
    return (
        adjoint.astype(ml_dtypes.bfloat16),
        high,
        low,
        np.cos(turn).astype(np.float32),
        np.sin(turn).astype(np.float32),
    )


def iteration_kernel(first, dims, *refs):
    chans, slots, blocks_per, rows, extent, tile = dims
    per_row = extent // tile
    cap = chans * slots * blocks_per
    refs = list(refs)
    ent, off = refs[:2]
    v_ref, tiles_ref, x_hbm, u_hbm, carry_ref = refs[2:7]
    refs = refs[7:]
    if not first:
        last_ref, tot_ref, rad_ref = refs[:3]
        refs = refs[3:]
    tables, (cos_ref, sin_ref) = refs[:3], refs[3:5]
    img_hbm, push_hbm, sum_ref, seen_ref, ef_ref, el_ref, pl_ref = refs[5:12]
    big, g_re, g_im, ph_c, ph_s, bacc, ebuf, tbuf, sems = refs[12:21]
    adj_ref, hi_ref, lo_ref, table_sems = refs[21:25]
    x_in, u_in, x_out, u_out, in_sems, out_sems = refs[25:31]
    if not first:
        us, scale = refs[31:33]
    c = pl.program_id(0)
    total = off[chans]
    groups = lax.shift_right_logical(total + (GROUP - 1), GROUP.bit_length() - 1)
    chunks = sum(
        (total > begin).astype(jnp.int32) for begin in range(0, cap, CHUNK)
    )
    slot = lax.rem(c, DEPTH)
    x_ref, u_ref = x_in.at[pl.ds(slot, 1)], u_in.at[pl.ds(slot, 1)]
    img_ref, push_ref = x_out.at[pl.ds(slot, 1)], u_out.at[pl.ds(slot, 1)]

    def entry(q):
        where_it_goes, source = split_divide(ent[q], cap)
        row, block = split_divide(where_it_goes, per_row)
        return source, row, block

    def issue(group):
        slot = lax.rem(group, RING)
        for t in range(GROUP):
            source, _, _ = entry(group * GROUP + t)
            pltpu.make_async_copy(
                tiles_ref.at[source], tbuf.at[slot * GROUP + t], sems.at[slot]
            ).start()

    def await_group(group):
        slot = lax.rem(group, RING)
        pltpu.make_async_copy(
            tiles_ref.at[pl.ds(0, GROUP)], tbuf.at[pl.ds(slot * GROUP, GROUP)], sems.at[slot]
        ).wait()
        return slot * GROUP

    def prime():
        @pl.loop(0, jnp.minimum(groups, RING))
        def _(group):
            issue(group)

    def copies_in(channel):
        place = lax.rem(channel, DEPTH)
        return (
            pltpu.make_async_copy(x_hbm.at[channel], x_in.at[place], in_sems.at[0, place]),
            pltpu.make_async_copy(u_hbm.at[channel], u_in.at[place], in_sems.at[1, place]),
        )

    def copies_out(channel):
        place = lax.rem(channel, DEPTH)
        return (
            pltpu.make_async_copy(x_out.at[place], img_hbm.at[channel], out_sems.at[0, place]),
            pltpu.make_async_copy(u_out.at[place], push_hbm.at[channel], out_sems.at[1, place]),
        )

    def table_copy(k):
        return pltpu.make_async_copy(tables[k], (adj_ref, hi_ref, lo_ref)[k], table_sems.at[k])

    def widen(value):
        return jnp.concatenate([value] * (PIECE // tile), axis=1)

    @pl.when(c == 0)
    def _():
        prime()
        for k in range(3):
            table_copy(k).start()
        for channel in range(min(DEPTH, chans)):
            for copy in copies_in(jnp.int32(channel)):
                copy.start()
        sum_ref[...] = jnp.zeros_like(sum_ref)
        if not first:
            for band in range(2):
                for r in range(0, rows, 8):
                    norms = jnp.sqrt(tot_ref[band, r : r + 8] + 1e-06)
                    scale[band, r : r + 8] = jnp.minimum(1.0, rad_ref[r : r + 8] / norms)

        @pl.loop(0, groups)
        def _(group):
            base = await_group(group)
            re, im, co, si = [], [], [], []
            for t in range(GROUP):
                source, _, block = entry(group * GROUP + t)
                place, _ = split_divide(source, blocks_per)
                weights = v_ref[place].astype(jnp.bfloat16)
                contrib = jnp.dot(weights, tbuf[base + t], preferred_element_type=jnp.float32)
                re.append(contrib[0:1])
                im.append(contrib[1:2])
                co.append(cos_ref[pl.ds(block, 1), :])
                si.append(sin_ref[pl.ds(block, 1), :])
            at = pl.ds(pl.multiple_of(group * GROUP, GROUP), GROUP)
            g_re[at, :] = jnp.concatenate(re, axis=0)
            g_im[at, :] = jnp.concatenate(im, axis=0)
            ph_c[at, :] = jnp.concatenate(co, axis=0)
            ph_s[at, :] = jnp.concatenate(si, axis=0)

            @pl.when(group + RING < groups)
            def _():
                issue(group + RING)

        table_copy(0).wait()

        @pl.loop(0, chunks)
        def _(chunk):
            at = pl.ds(pl.multiple_of(chunk * CHUNK, CHUNK), CHUNK)
            lhs = jnp.concatenate([g_re[at, :], g_im[at, :]], axis=1).astype(jnp.bfloat16)
            turn_c, turn_s = widen(ph_c[at, :]), widen(ph_s[at, :])
            for j in range(0, extent, PIECE):
                even = jnp.dot(lhs, adj_ref[:, j : j + PIECE], preferred_element_type=jnp.float32)
                odd = jnp.dot(
                    lhs,
                    adj_ref[:, extent + j : extent + j + PIECE],
                    preferred_element_type=jnp.float32,
                )
                big[at, j : j + PIECE] = turn_c * even - turn_s * odd

        pl.when(groups > RING)(prime)

    start, end = off[c], off[c + 1]
    bacc[...] = jnp.zeros_like(bacc)

    @pl.loop(start, end)
    def _(q):
        _, row, _ = entry(q)
        bacc[pl.ds(row, 1), :] += big[pl.ds(q, 1), :]

    for copy in copies_in(c):
        copy.wait()

    @pl.when(c >= DEPTH)
    def _():
        for copy in copies_out(c - DEPTH):
            copy.wait()

    if not first:
        us[0, 7:8] = carry_ref[pl.ds(c, 1), :]
        for band in range(2):
            for r in range(0, rows, 8):
                value = u_ref[0, band, r : r + 8]
                if band == 0 and r == rows - 8:
                    value = jnp.concatenate([value[:7], last_ref[pl.ds(c, 1), :]], axis=0)
                us[band, r + 8 : r + 16] = value * scale[band, r : r + 8]

    def dual(band, r):
        return u_ref[0, band, r : r + 8] if first else us[band, r + 8 : r + 16]

    def dual_above(r):
        if not first:
            return us[0, r + 7 : r + 15]
        if r:
            return u_ref[0, 0, r - 1 : r + 7]
        return jnp.concatenate([carry_ref[pl.ds(c, 1), :], u_ref[0, 0, 0:7]], axis=0)

    column = lax.broadcasted_iota(jnp.int32, (8, extent), 1)
    for r in range(0, rows, 8):
        across = dual(1, r)
        leftward = jnp.where(column == 0, 0.0, pltpu.roll(across, 1, 1))
        synthesis = (dual_above(r) - dual(0, r) + leftward - across) * ROOT_HALF
        image = x_ref[0, r : r + 8]
        image_next = jnp.maximum(image - STEP_PRIMAL * (synthesis + bacc[r : r + 8]), 0.0)
        img_ref[0, r : r + 8] = image_next
        ebuf[r : r + 8] = 2.0 * image_next - image
    ebuf[rows : rows + 8] = jnp.zeros((8, extent), jnp.float32)

    @pl.loop(start, end)
    def _(q):
        _, row, _ = entry(q)
        big[pl.ds(q, 1), :] = ebuf[pl.ds(row, 1), :]

    for r in range(0, rows, 8):
        here = ebuf[r : r + 8]
        below = ebuf[r + 1 : r + 9]
        right = jnp.where(column == extent - 1, 0.0, pltpu.roll(here, extent - 1, 1))
        vertical = dual(0, r) + (STEP_PRIOR * ROOT_HALF) * (below - here)
        horizontal = dual(1, r) + (STEP_PRIOR * ROOT_HALF) * (right - here)
        if push_ref.dtype == jnp.float32:
            push_ref[0, 0, r : r + 8] = vertical
            push_ref[0, 1, r : r + 8] = horizontal
        elif r % 16 == 0:
            upper = vertical, horizontal
        else:
            for band, value in enumerate((vertical, horizontal)):
                pair = jnp.concatenate([upper[band], value], axis=0)
                push_ref[0, band, r - 8 : r + 8] = pair.astype(push_ref.dtype)
        sum_ref[0, r : r + 8] += vertical * vertical
        sum_ref[1, r : r + 8] += horizontal * horizontal
        if r == rows - 8:
            pl_ref[pl.ds(c, 1), :] = vertical[7:8]
    for copy in copies_out(c):
        copy.start()

    @pl.when(c + DEPTH < chans)
    def _():
        for copy in copies_in(c + DEPTH):
            copy.start()

    ef_ref[pl.ds(c, 1), :] = ebuf[0:1]
    el_ref[pl.ds(c, 1), :] = ebuf[rows - 1 : rows]

    @pl.when(c == chans - 1)
    def _():
        seen_ref[...] = jnp.zeros_like(seen_ref)
        table_copy(1).wait()
        table_copy(2).wait()

        @pl.loop(0, chunks)
        def _(chunk):
            at = pl.ds(pl.multiple_of(chunk * CHUNK, CHUNK), CHUNK)
            turn_c, turn_s = widen(ph_c[at, :]), widen(ph_s[at, :])
            grid = jnp.zeros((CHUNK, 2 * tile), jnp.float32)
            for j in range(0, extent, PIECE):
                value = big[at, j : j + PIECE].astype(jnp.bfloat16).astype(jnp.float32)
                for turn, base in ((turn_c, j), (turn_s, extent + j)):
                    turned = value * turn
                    high = turned.astype(jnp.bfloat16)
                    low = (turned - high.astype(jnp.float32)).astype(jnp.bfloat16)
                    table = hi_ref[base : base + PIECE, :]
                    grid += jnp.dot(high, table, preferred_element_type=jnp.float32)
                    grid += jnp.dot(low, table, preferred_element_type=jnp.float32)
                    grid += jnp.dot(
                        high, lo_ref[base : base + PIECE, :], preferred_element_type=jnp.float32
                    )
            g_re[at, :] = grid[:, :tile]
            g_im[at, :] = grid[:, tile:]

        @pl.loop(0, groups)
        def _(group):
            base = lax.rem(group, RING) * GROUP

            @pl.when(groups > RING)
            def _():
                await_group(group)

            at = pl.ds(pl.multiple_of(group * GROUP, GROUP), GROUP)
            lhs = jnp.concatenate([g_re[at, :], g_im[at, :]], axis=0).astype(jnp.bfloat16)
            for t in range(GROUP):
                q = group * GROUP + t
                source, _, _ = entry(q)
                place, _ = split_divide(source, blocks_per)
                part = lax.dot_general(
                    lhs, tbuf[base + t], (((1,), (1,)), ((), ())), preferred_element_type=jnp.float32
                )
                part = jnp.concatenate([part[t : t + 1], part[GROUP + t : GROUP + t + 1]], axis=0)
                seen_ref[place] += jnp.where(q < total, part, 0.0)

            @pl.when(group + RING < groups)
            def _():
                issue(group + RING)

        for channel in range(max(chans - DEPTH, 0), chans):
            for copy in copies_out(jnp.int32(channel)):
                copy.wait()


def iteration(first, final, tables, ent, off, v, tiles, x, u, carry, extra=()):
    chans, rows, extent = x.shape
    tile = tiles.shape[-1]
    slots = v.shape[0] // chans
    blocks_per = tiles.shape[0] // v.shape[0]
    cap = ent.shape[0]
    dims = (chans, slots, blocks_per, rows, extent, tile)

    def whole(shape):
        return pl.BlockSpec(shape, lambda c, *_: (0,) * len(shape), pipeline_mode=pl.Buffered(1))

    outs = [x.shape, u.shape, (2, rows, extent), v.shape] + [(chans, extent)] * 3
    push_type = jnp.bfloat16 if final and rows % 16 == 0 else jnp.float32
    rows_cap = pl.cdiv(cap, CHUNK) * CHUNK
    scratch = [
        pltpu.VMEM((rows_cap, extent), jnp.float32),
        pltpu.VMEM((rows_cap, tile), jnp.float32),
        pltpu.VMEM((rows_cap, tile), jnp.float32),
        pltpu.VMEM((rows_cap, tile), jnp.float32),
        pltpu.VMEM((rows_cap, tile), jnp.float32),
        pltpu.VMEM((rows, extent), jnp.float32),
        pltpu.VMEM((rows + 8, extent), jnp.float32),
        pltpu.VMEM((RING * GROUP, tile, tile), jnp.bfloat16),
        pltpu.SemaphoreType.DMA((RING,)),
        *(pltpu.VMEM(t.shape, t.dtype) for t in tables[:3]),
        pltpu.SemaphoreType.DMA((3,)),
        pltpu.VMEM((DEPTH, rows, extent), jnp.float32),
        pltpu.VMEM((DEPTH, 2, rows, extent), jnp.float32),
        pltpu.VMEM((DEPTH, rows, extent), jnp.float32),
        pltpu.VMEM((DEPTH, 2, rows, extent), push_type),
        *[pltpu.SemaphoreType.DMA((2, DEPTH))] * 2,
    ]
    if not first:
        scratch += [
            pltpu.VMEM((2, rows + 8, extent), jnp.float32),
            pltpu.VMEM((2, rows, extent), jnp.float32),
        ]
    pin = lambda a: pltpu.with_memory_space_constraint(a, pltpu.HBM)
    x, u, tiles = pin(x), pin(u), pin(tiles)
    v = pin(v) if first else v
    tables = [pin(t) for t in tables]
    in_hbm = pl.BlockSpec(memory_space=pltpu.HBM)
    operands = [v, tiles, x, u, carry, *extra, *tables]
    in_specs = [whole(v.shape), in_hbm, in_hbm, in_hbm]
    in_specs += [whole(a.shape) for a in (carry, *extra)] + [in_hbm] * 3
    in_specs += [whole(a.shape) for a in tables[3:]]
    return pl.pallas_call(
        functools.partial(iteration_kernel, first, dims),
        out_shape=[
            pltpu.HBM(s, push_type if k == 1 else jnp.float32) if k < 2 else jax.ShapeDtypeStruct(s, jnp.float32)
            for k, s in enumerate(outs)
        ],
        grid_spec=pltpu.PrefetchScalarGridSpec(
            num_scalar_prefetch=2,
            grid=(chans,),
            in_specs=in_specs,
            out_specs=[in_hbm] * 2 + [pl.BlockSpec(s, lambda c, *_, n=len(s): (0,) * n) for s in outs[2:]],
            scratch_shapes=scratch,
        ),
        compiler_params=pltpu.CompilerParams(
            dimension_semantics=("arbitrary",), vmem_limit_bytes=46 << 20
        ),
        name="primal_dual_first" if first else "primal_dual_next",
    )(ent, off, *operands)


def shrink_kernel(push_ref, last_ref, tot_ref, rad_ref, out_ref, scale):
    rows = push_ref.shape[2]
    c = pl.program_id(0)

    @pl.when(c == 0)
    def _():
        for band in range(2):
            for r in range(0, rows, 8):
                norms = jnp.sqrt(tot_ref[band, r : r + 8] + 1e-06)
                scale[band, r : r + 8] = jnp.minimum(1.0, rad_ref[r : r + 8] / norms)

    strip = 16 if rows % 16 == 0 else 8
    for band in range(2):
        for r in range(0, rows, strip):
            value = push_ref[0, band, r : r + strip].astype(jnp.float32)
            if band == 0 and r == rows - strip:
                value = jnp.concatenate([value[:-1], last_ref[pl.ds(c, 1), :]], axis=0)
            out_ref[0, band, r : r + strip] = value * scale[band, r : r + strip]


def shrink(push, last, total, radius):
    chans, _, rows, extent = push.shape

    def whole(shape):
        return pl.BlockSpec(shape, lambda c: (0,) * len(shape), pipeline_mode=pl.Buffered(1))

    dual_spec = pl.BlockSpec((1, 2, rows, extent), lambda c: (c, 0, 0, 0))
    return pl.pallas_call(
        shrink_kernel,
        out_shape=jax.ShapeDtypeStruct(push.shape, jnp.float32),
        grid=(chans,),
        in_specs=[dual_spec, whole(last.shape), whole(total.shape), whole(radius.shape)],
        out_specs=dual_spec,
        scratch_shapes=[pltpu.VMEM((2, rows, extent), jnp.float32)],
        compiler_params=pltpu.CompilerParams(
            dimension_semantics=("arbitrary",), vmem_limit_bytes=8 << 20
        ),
        name="shrink",
    )(push, last, total, radius)


def exchange(value, axis, bit):
    count = lax.axis_size(axis)
    return lax.ppermute(value, axis, [(i, i ^ bit) for i in range(count)])


def halve(value, axis, bits):
    index = lax.axis_index(axis)
    for bit in bits:
        half = value.shape[0] // 2
        mine = (index // bit) % 2
        keep = lax.dynamic_slice_in_dim(value, mine * half, half, 0)
        send = lax.dynamic_slice_in_dim(value, (1 - mine) * half, half, 0)
        value = keep + exchange(send, axis, bit)
    return value


def double(value, axis, bits):
    index = lax.axis_index(axis)
    for bit in reversed(bits):
        other = exchange(value, axis, bit)
        first = (index // bit) % 2 == 0
        value = jnp.concatenate(
            [jnp.where(first, value, other), jnp.where(first, other, value)], axis=0
        )
    return value


def shard_of(value, axis, bits):
    index = lax.axis_index(axis)
    for bit in bits:
        half = value.shape[0] // 2
        value = lax.dynamic_slice_in_dim(value, ((index // bit) % 2) * half, half, 0)
    return value


def sum_over_channels(local_sum):
    count = lax.axis_size("chan")
    bands, rows, extent = local_sum.shape
    if count & (count - 1) or count < 2 or (bands * rows) % count:
        return lax.psum(local_sum, "chan")
    chips = count // 2
    index = lax.axis_index("chan") // 2
    value = halve(local_sum.reshape(bands * rows, extent), "chan", [1])
    value = value.reshape(chips, -1, extent)
    take = lambda at: lax.dynamic_index_in_dim(value, at, 0, False)
    parts = [exchange(take(index ^ d), "chan", 2 * d) for d in range(1, chips)]
    total = sum(parts, take(index))
    sums = [total] + [exchange(total, "chan", 2 * d) for d in range(1, chips)]
    placed = []
    for place in range(chips):
        chosen = sums[0]
        for d in range(1, chips):
            chosen = jnp.where((index ^ place) == d, sums[d], chosen)
        placed.append(chosen)
    value = double(jnp.concatenate(placed, axis=0), "chan", [1])
    return value.reshape(bands, rows, extent)


def update_data(seen, data_dual, observed, live):
    count = lax.axis_size("facet")
    if count & (count - 1) or seen.shape[0] % count:
        seen = lax.psum(seen, "facet")
        return (data_dual + STEP_DATA * (seen - observed)) * live / (1.0 + STEP_DATA)
    bits = [1 << k for k in range(count.bit_length() - 1)]
    seen = halve(seen, "facet", bits)
    data_dual, observed, live = (shard_of(a, "facet", bits) for a in (data_dual, observed, live))
    fresh = (data_dual + STEP_DATA * (seen - observed)) * live / (1.0 + STEP_DATA)
    return double(fresh, "facet", bits)


def local(x_init, u_init, v_init, observed, tiles, pattern, counts, facet_bounds):
    chans, rows, extent = x_init.shape
    slots, blocks_per = pattern.shape[1:]
    tile = tiles.shape[-1]
    per_row = extent // tile
    facet = lax.axis_index("facet")
    row_start = facet * rows
    cap = chans * slots * blocks_per
    tables = [jnp.asarray(t) for t in transform_tables(extent, tile)]

    live = jnp.arange(slots, dtype=jnp.int32)[None, :] < counts[:, None]
    local_index = pattern - row_start * per_row
    keep = (local_index >= 0) & (local_index < rows * per_row) & live[:, :, None]
    keep = keep.reshape(cap)
    order = jnp.arange(cap, dtype=jnp.int32)
    ahead = jnp.sum(
        (keep[None, :] & (order[None, :] < order[:, None])).astype(jnp.int32), axis=1
    )
    packed = jnp.where(keep, local_index.reshape(cap) * cap + order, 0)
    ent = jnp.sum(
        jnp.where(keep[None, :] & (ahead[None, :] == order[:, None]), packed[None, :], 0), axis=1
    )
    kept = jnp.sum(keep.reshape(chans, -1).astype(jnp.int32), axis=1)
    edges = jnp.arange(chans + 1, dtype=jnp.int32)
    off = jnp.sum(jnp.where(edges[None, :chans] < edges[:, None], kept[None, :], 0), axis=1)

    row_ids = row_start - 1 + jnp.arange(rows + 1, dtype=jnp.int32)
    inside = (row_ids[None, :] >= facet_bounds[:, 0:1]) & (row_ids[None, :] < facet_bounds[:, 1:2])
    cover = jnp.sum(inside.astype(jnp.float32), axis=0)
    radius = (RADIUS / cover)[:, None]
    radius, radius_above = radius[1:], radius[0]

    live_float = jnp.broadcast_to(live.reshape(-1, 1, 1).astype(jnp.float32), (chans * slots, 1, 1))
    observed = observed.reshape(chans * slots, 2, tile)
    data_dual = v_init.reshape(chans * slots, 2, tile)
    tiles = tiles.reshape(cap, tile, tile)
    image, dual = x_init, u_init
    carry = shifted(u_init[:, 0, -1, :], "facet", 1)
    extra = ()
    for rounds in range(ITERS):
        image, dual, local_sum, seen, first_row, last_row, pushed_last = iteration(
            rounds == 0, rounds == ITERS - 1, tables, ent, off, data_dual, tiles, image, dual, carry, extra
        )
        half_step = STEP_PRIOR * ROOT_HALF
        pushed_last = pushed_last + half_step * shifted(first_row, "facet", -1)
        local_sum = lax.dynamic_update_slice(
            local_sum, jnp.sum(pushed_last * pushed_last, axis=0)[None, None], (0, rows - 1, 0)
        )
        total = sum_over_channels(local_sum)
        data_dual = update_data(seen, data_dual, observed, live_float)
        extra = (pushed_last, total, radius)
        if rounds + 1 < ITERS:
            above = carry + half_step * (first_row - shifted(last_row, "facet", 1))
            norms = jnp.sqrt(shifted(total[0, rows - 1 :], "facet", 1) + 1e-06)
            carry = jnp.where(facet > 0, above * jnp.minimum(1.0, radius_above / norms), 0.0)
    return (
        image,
        shrink(dual, *extra),
        data_dual.reshape(v_init.shape),
    )


def solution(mesh):
    in_specs = (
        P("chan", "facet", None),
        P("chan", None, "facet", None),
        P("chan", None, None, None),
        P("chan", None, None, None),
        P("chan", None, None, None, None),
        P("chan", None, None),
        P("chan"),
        P(),
    )
    out_specs = (
        P("chan", "facet", None),
        P("chan", None, "facet", None),
        P("chan", None, None, None),
    )
    return jax.shard_map(local, mesh=mesh, in_specs=in_specs, out_specs=out_specs, check_vma=False)
```

```python
import functools
import math

import jax
import jax.numpy as jnp
import ml_dtypes
import numpy as np
from jax import lax
from jax.experimental import pallas as pl
from jax.experimental.pallas import tpu as pltpu
from jax.sharding import PartitionSpec as P

ITERS = 2

STEP_PRIMAL = 0.5
STEP_PRIOR = 0.5
STEP_DATA = 1.0
RADIUS = 12.0
ROOT_HALF = 0.7071067811865476

GROUP = 16
RING = 18
CHUNK = 352
PIECE = 512
DEPTH = 3


def shifted(shard, axis, by):
    count = lax.axis_size(axis)
    pairs = [(i, i + by) for i in range(count) if 0 <= i + by < count]
    return lax.ppermute(shard, axis, pairs)


def split_divide(value, by):
    if by & (by - 1) == 0:
        return lax.shift_right_logical(value, by.bit_length() - 1), value & (by - 1)
    return value // by, value % by


def transform_tables(extent, tile):
    j = np.arange(extent, dtype=np.int64)
    g = np.arange(tile, dtype=np.int64)
    angle = (g[:, None] * j[None, :] % extent) * (2.0 * math.pi / extent)
    cos, sin = np.cos(angle) / math.sqrt(extent), np.sin(angle) / math.sqrt(extent)
    adjoint = np.concatenate(
        [np.concatenate([cos, sin], 1), np.concatenate([-sin, cos], 1)], 0
    )
    forward = np.concatenate(
        [np.concatenate([cos.T, -sin.T], 1), np.concatenate([-sin.T, -cos.T], 1)], 0
    )
    high = forward.astype(ml_dtypes.bfloat16)
    low = (forward - high.astype(np.float64)).astype(ml_dtypes.bfloat16)
    blocks = extent // tile
    turn = (np.arange(blocks)[:, None] * np.arange(tile)[None, :] % blocks) * (2.0 * math.pi / blocks)
    return (
        adjoint.astype(ml_dtypes.bfloat16),
        high,
        low,
        np.cos(turn).astype(np.float32),
        np.sin(turn).astype(np.float32),
    )


def iteration_kernel(first, dims, *refs):
    chans, slots, blocks_per, rows, extent, tile = dims
    per_row = extent // tile
    cap = chans * slots * blocks_per
    refs = list(refs)
    ent, off = refs[:2]
    v_ref, tiles_ref, x_hbm, u_hbm, carry_ref = refs[2:7]
    refs = refs[7:]
    if not first:
        last_ref, tot_ref, rad_ref = refs[:3]
        refs = refs[3:]
    tables, (cos_ref, sin_ref) = refs[:3], refs[3:5]
    img_hbm, push_hbm, sum_ref, seen_ref, ef_ref, el_ref, pl_ref = refs[5:12]
    big, g_re, g_im, ph_c, ph_s, bacc, ebuf, tbuf, sems = refs[12:21]
    adj_ref, hi_ref, lo_ref, table_sems = refs[21:25]
    x_in, u_in, x_out, u_out, in_sems, out_sems = refs[25:31]
    if not first:
        us, scale = refs[31:33]
    c = pl.program_id(0)
    total = off[chans]
    groups = lax.shift_right_logical(total + (GROUP - 1), GROUP.bit_length() - 1)
    chunks = sum(
        (total > begin).astype(jnp.int32) for begin in range(0, cap, CHUNK)
    )
    slot = lax.rem(c, DEPTH)
    x_ref, u_ref = x_in.at[pl.ds(slot, 1)], u_in.at[pl.ds(slot, 1)]
    img_ref, push_ref = x_out.at[pl.ds(slot, 1)], u_out.at[pl.ds(slot, 1)]

    def entry(q):
        where_it_goes, source = split_divide(ent[q], cap)
        row, block = split_divide(where_it_goes, per_row)
        return source, row, block

    def issue(group):
        slot = lax.rem(group, RING)
        for t in range(GROUP):
            source, _, _ = entry(group * GROUP + t)
            pltpu.make_async_copy(
                tiles_ref.at[source], tbuf.at[slot * GROUP + t], sems.at[slot]
            ).start()

    def await_group(group):
        slot = lax.rem(group, RING)
        pltpu.make_async_copy(
            tiles_ref.at[pl.ds(0, GROUP)], tbuf.at[pl.ds(slot * GROUP, GROUP)], sems.at[slot]
        ).wait()
        return slot * GROUP

    def prime():
        @pl.loop(0, jnp.minimum(groups, RING))
        def _(group):
            issue(group)

    def copies_in(channel):
        place = lax.rem(channel, DEPTH)
        return (
            pltpu.make_async_copy(x_hbm.at[channel], x_in.at[place], in_sems.at[0, place]),
            pltpu.make_async_copy(u_hbm.at[channel], u_in.at[place], in_sems.at[1, place]),
        )

    def copies_out(channel):
        place = lax.rem(channel, DEPTH)
        return (
            pltpu.make_async_copy(x_out.at[place], img_hbm.at[channel], out_sems.at[0, place]),
            pltpu.make_async_copy(u_out.at[place], push_hbm.at[channel], out_sems.at[1, place]),
        )

    def table_copy(k):
        return pltpu.make_async_copy(tables[k], (adj_ref, hi_ref, lo_ref)[k], table_sems.at[k])

    def widen(value):
        return jnp.concatenate([value] * (PIECE // tile), axis=1)

    @pl.when(c == 0)
    def _():
        prime()
        for k in range(3):
            table_copy(k).start()
        for channel in range(min(DEPTH, chans)):
            for copy in copies_in(jnp.int32(channel)):
                copy.start()
        sum_ref[...] = jnp.zeros_like(sum_ref)
        if not first:
            for band in range(2):
                for r in range(0, rows, 8):
                    norms = jnp.sqrt(tot_ref[band, r : r + 8] + 1e-06)
                    scale[band, r : r + 8] = jnp.minimum(1.0, rad_ref[r : r + 8] / norms)

        @pl.loop(0, groups)
        def _(group):
            base = await_group(group)
            re, im, co, si = [], [], [], []
            for t in range(GROUP):
                source, _, block = entry(group * GROUP + t)
                place, _ = split_divide(source, blocks_per)
                weights = v_ref[place].astype(jnp.bfloat16)
                contrib = jnp.dot(weights, tbuf[base + t], preferred_element_type=jnp.float32)
                re.append(contrib[0:1])
                im.append(contrib[1:2])
                co.append(cos_ref[pl.ds(block, 1), :])
                si.append(sin_ref[pl.ds(block, 1), :])
            at = pl.ds(pl.multiple_of(group * GROUP, GROUP), GROUP)
            g_re[at, :] = jnp.concatenate(re, axis=0)
            g_im[at, :] = jnp.concatenate(im, axis=0)
            ph_c[at, :] = jnp.concatenate(co, axis=0)
            ph_s[at, :] = jnp.concatenate(si, axis=0)

            @pl.when(group + RING < groups)
            def _():
                issue(group + RING)

        table_copy(0).wait()

        @pl.loop(0, chunks)
        def _(chunk):
            at = pl.ds(pl.multiple_of(chunk * CHUNK, CHUNK), CHUNK)
            lhs = jnp.concatenate([g_re[at, :], g_im[at, :]], axis=1).astype(jnp.bfloat16)
            turn_c, turn_s = widen(ph_c[at, :]), widen(ph_s[at, :])
            for j in range(0, extent, PIECE):
                even = jnp.dot(lhs, adj_ref[:, j : j + PIECE], preferred_element_type=jnp.float32)
                odd = jnp.dot(
                    lhs,
                    adj_ref[:, extent + j : extent + j + PIECE],
                    preferred_element_type=jnp.float32,
                )
                big[at, j : j + PIECE] = turn_c * even - turn_s * odd

        pl.when(groups > RING)(prime)

    start, end = off[c], off[c + 1]
    bacc[...] = jnp.zeros_like(bacc)

    @pl.loop(start, end)
    def _(q):
        _, row, _ = entry(q)
        bacc[pl.ds(row, 1), :] += big[pl.ds(q, 1), :]

    for copy in copies_in(c):
        copy.wait()

    @pl.when(c >= DEPTH)
    def _():
        for copy in copies_out(c - DEPTH):
            copy.wait()

    if not first:
        us[0, 7:8] = carry_ref[pl.ds(c, 1), :]
        for band in range(2):
            for r in range(0, rows, 8):
                value = u_ref[0, band, r : r + 8]
                if band == 0 and r == rows - 8:
                    value = jnp.concatenate([value[:7], last_ref[pl.ds(c, 1), :]], axis=0)
                us[band, r + 8 : r + 16] = value * scale[band, r : r + 8]

    def dual(band, r):
        return u_ref[0, band, r : r + 8] if first else us[band, r + 8 : r + 16]

    def dual_above(r):
        if not first:
            return us[0, r + 7 : r + 15]
        if r:
            return u_ref[0, 0, r - 1 : r + 7]
        return jnp.concatenate([carry_ref[pl.ds(c, 1), :], u_ref[0, 0, 0:7]], axis=0)

    column = lax.broadcasted_iota(jnp.int32, (8, extent), 1)
    for r in range(0, rows, 8):
        across = dual(1, r)
        leftward = jnp.where(column == 0, 0.0, pltpu.roll(across, 1, 1))
        synthesis = (dual_above(r) - dual(0, r) + leftward - across) * ROOT_HALF
        image = x_ref[0, r : r + 8]
        image_next = jnp.maximum(image - STEP_PRIMAL * (synthesis + bacc[r : r + 8]), 0.0)
        img_ref[0, r : r + 8] = image_next
        ebuf[r : r + 8] = 2.0 * image_next - image
    ebuf[rows : rows + 8] = jnp.zeros((8, extent), jnp.float32)

    @pl.loop(start, end)
    def _(q):
        _, row, _ = entry(q)
        big[pl.ds(q, 1), :] = ebuf[pl.ds(row, 1), :]

    for r in range(0, rows, 8):
        here = ebuf[r : r + 8]
        below = ebuf[r + 1 : r + 9]
        right = jnp.where(column == extent - 1, 0.0, pltpu.roll(here, extent - 1, 1))
        vertical = dual(0, r) + (STEP_PRIOR * ROOT_HALF) * (below - here)
        horizontal = dual(1, r) + (STEP_PRIOR * ROOT_HALF) * (right - here)
        if push_ref.dtype == jnp.float32:
            push_ref[0, 0, r : r + 8] = vertical
            push_ref[0, 1, r : r + 8] = horizontal
        elif r % 16 == 0:
            upper = vertical, horizontal
        else:
            for band, value in enumerate((vertical, horizontal)):
                pair = jnp.concatenate([upper[band], value], axis=0)
                push_ref[0, band, r - 8 : r + 8] = pair.astype(push_ref.dtype)
        sum_ref[0, r : r + 8] += vertical * vertical
        sum_ref[1, r : r + 8] += horizontal * horizontal
        if r == rows - 8:
            pl_ref[pl.ds(c, 1), :] = vertical[7:8]
    for copy in copies_out(c):
        copy.start()

    @pl.when(c + DEPTH < chans)
    def _():
        for copy in copies_in(c + DEPTH):
            copy.start()

    ef_ref[pl.ds(c, 1), :] = ebuf[0:1]
    el_ref[pl.ds(c, 1), :] = ebuf[rows - 1 : rows]

    @pl.when(c == chans - 1)
    def _():
        seen_ref[...] = jnp.zeros_like(seen_ref)
        table_copy(1).wait()
        table_copy(2).wait()

        @pl.loop(0, chunks)
        def _(chunk):
            at = pl.ds(pl.multiple_of(chunk * CHUNK, CHUNK), CHUNK)
            turn_c, turn_s = widen(ph_c[at, :]), widen(ph_s[at, :])
            grid = jnp.zeros((CHUNK, 2 * tile), jnp.float32)
            for j in range(0, extent, PIECE):
                value = big[at, j : j + PIECE].astype(jnp.bfloat16).astype(jnp.float32)
                for turn, base in ((turn_c, j), (turn_s, extent + j)):
                    turned = value * turn
                    high = turned.astype(jnp.bfloat16)
                    low = (turned - high.astype(jnp.float32)).astype(jnp.bfloat16)
                    table = hi_ref[base : base + PIECE, :]
                    grid += jnp.dot(high, table, preferred_element_type=jnp.float32)
                    grid += jnp.dot(low, table, preferred_element_type=jnp.float32)
                    grid += jnp.dot(
                        high, lo_ref[base : base + PIECE, :], preferred_element_type=jnp.float32
                    )
            g_re[at, :] = grid[:, :tile]
            g_im[at, :] = grid[:, tile:]

        @pl.loop(0, groups)
        def _(group):
            base = lax.rem(group, RING) * GROUP

            @pl.when(groups > RING)
            def _():
                await_group(group)

            at = pl.ds(pl.multiple_of(group * GROUP, GROUP), GROUP)
            lhs = jnp.concatenate([g_re[at, :], g_im[at, :]], axis=0).astype(jnp.bfloat16)
            for t in range(GROUP):
                q = group * GROUP + t
                source, _, _ = entry(q)
                place, _ = split_divide(source, blocks_per)
                part = lax.dot_general(
                    lhs, tbuf[base + t], (((1,), (1,)), ((), ())), preferred_element_type=jnp.float32
                )
                part = jnp.concatenate([part[t : t + 1], part[GROUP + t : GROUP + t + 1]], axis=0)
                seen_ref[place] += jnp.where(q < total, part, 0.0)

            @pl.when(group + RING < groups)
            def _():
                issue(group + RING)

        for channel in range(max(chans - DEPTH, 0), chans):
            for copy in copies_out(jnp.int32(channel)):
                copy.wait()


def iteration(first, final, tables, ent, off, v, tiles, x, u, carry, extra=()):
    chans, rows, extent = x.shape
    tile = tiles.shape[-1]
    slots = v.shape[0] // chans
    blocks_per = tiles.shape[0] // v.shape[0]
    cap = ent.shape[0]
    dims = (chans, slots, blocks_per, rows, extent, tile)

    def whole(shape):
        return pl.BlockSpec(shape, lambda c, *_: (0,) * len(shape), pipeline_mode=pl.Buffered(1))

    outs = [x.shape, u.shape, (2, rows, extent), v.shape] + [(chans, extent)] * 3
    push_type = jnp.bfloat16 if final and rows % 16 == 0 else jnp.float32
    rows_cap = pl.cdiv(cap, CHUNK) * CHUNK
    scratch = [
        pltpu.VMEM((rows_cap, extent), jnp.float32),
        pltpu.VMEM((rows_cap, tile), jnp.float32),
        pltpu.VMEM((rows_cap, tile), jnp.float32),
        pltpu.VMEM((rows_cap, tile), jnp.float32),
        pltpu.VMEM((rows_cap, tile), jnp.float32),
        pltpu.VMEM((rows, extent), jnp.float32),
        pltpu.VMEM((rows + 8, extent), jnp.float32),
        pltpu.VMEM((RING * GROUP, tile, tile), jnp.bfloat16),
        pltpu.SemaphoreType.DMA((RING,)),
        *(pltpu.VMEM(t.shape, t.dtype) for t in tables[:3]),
        pltpu.SemaphoreType.DMA((3,)),
        pltpu.VMEM((DEPTH, rows, extent), jnp.float32),
        pltpu.VMEM((DEPTH, 2, rows, extent), jnp.float32),
        pltpu.VMEM((DEPTH, rows, extent), jnp.float32),
        pltpu.VMEM((DEPTH, 2, rows, extent), push_type),
        *[pltpu.SemaphoreType.DMA((2, DEPTH))] * 2,
    ]
    if not first:
        scratch += [
            pltpu.VMEM((2, rows + 8, extent), jnp.float32),
            pltpu.VMEM((2, rows, extent), jnp.float32),
        ]
    pin = lambda a: pltpu.with_memory_space_constraint(a, pltpu.HBM)
    x, u, tiles = pin(x), pin(u), pin(tiles)
    v = pin(v) if first else v
    tables = [pin(t) for t in tables]
    in_hbm = pl.BlockSpec(memory_space=pltpu.HBM)
    operands = [v, tiles, x, u, carry, *extra, *tables]
    in_specs = [whole(v.shape), in_hbm, in_hbm, in_hbm]
    in_specs += [whole(a.shape) for a in (carry, *extra)] + [in_hbm] * 3
    in_specs += [whole(a.shape) for a in tables[3:]]
    return pl.pallas_call(
        functools.partial(iteration_kernel, first, dims),
        out_shape=[
            pltpu.HBM(s, push_type if k == 1 else jnp.float32) if k < 2 else jax.ShapeDtypeStruct(s, jnp.float32)
            for k, s in enumerate(outs)
        ],
        grid_spec=pltpu.PrefetchScalarGridSpec(
            num_scalar_prefetch=2,
            grid=(chans,),
            in_specs=in_specs,
            out_specs=[in_hbm] * 2 + [pl.BlockSpec(s, lambda c, *_, n=len(s): (0,) * n) for s in outs[2:]],
            scratch_shapes=scratch,
        ),
        compiler_params=pltpu.CompilerParams(
            dimension_semantics=("arbitrary",), vmem_limit_bytes=46 << 20
        ),
        name="primal_dual_first" if first else "primal_dual_next",
    )(ent, off, *operands)


def shrink_kernel(push_ref, last_ref, tot_ref, rad_ref, out_ref, scale):
    rows = push_ref.shape[2]
    c = pl.program_id(0)

    @pl.when(c == 0)
    def _():
        for band in range(2):
            for r in range(0, rows, 8):
                norms = jnp.sqrt(tot_ref[band, r : r + 8] + 1e-06)
                scale[band, r : r + 8] = jnp.minimum(1.0, rad_ref[r : r + 8] / norms)

    strip = 16 if rows % 16 == 0 else 8
    for band in range(2):
        for r in range(0, rows, strip):
            value = push_ref[0, band, r : r + strip].astype(jnp.float32)
            if band == 0 and r == rows - strip:
                value = jnp.concatenate([value[:-1], last_ref[pl.ds(c, 1), :]], axis=0)
            out_ref[0, band, r : r + strip] = value * scale[band, r : r + strip]


def shrink(push, last, total, radius):
    chans, _, rows, extent = push.shape

    def whole(shape):
        return pl.BlockSpec(shape, lambda c: (0,) * len(shape), pipeline_mode=pl.Buffered(1))

    dual_spec = pl.BlockSpec((1, 2, rows, extent), lambda c: (c, 0, 0, 0))
    return pl.pallas_call(
        shrink_kernel,
        out_shape=jax.ShapeDtypeStruct(push.shape, jnp.float32),
        grid=(chans,),
        in_specs=[dual_spec, whole(last.shape), whole(total.shape), whole(radius.shape)],
        out_specs=dual_spec,
        scratch_shapes=[pltpu.VMEM((2, rows, extent), jnp.float32)],
        compiler_params=pltpu.CompilerParams(
            dimension_semantics=("arbitrary",), vmem_limit_bytes=8 << 20
        ),
        name="shrink",
    )(push, last, total, radius)


def exchange(value, axis, bit):
    count = lax.axis_size(axis)
    return lax.ppermute(value, axis, [(i, i ^ bit) for i in range(count)])


def halve(value, axis, bits):
    index = lax.axis_index(axis)
    for bit in bits:
        half = value.shape[0] // 2
        mine = (index // bit) % 2
        keep = lax.dynamic_slice_in_dim(value, mine * half, half, 0)
        send = lax.dynamic_slice_in_dim(value, (1 - mine) * half, half, 0)
        value = keep + exchange(send, axis, bit)
    return value


def double(value, axis, bits):
    index = lax.axis_index(axis)
    for bit in reversed(bits):
        other = exchange(value, axis, bit)
        first = (index // bit) % 2 == 0
        value = jnp.concatenate(
            [jnp.where(first, value, other), jnp.where(first, other, value)], axis=0
        )
    return value


def shard_of(value, axis, bits):
    index = lax.axis_index(axis)
    for bit in bits:
        half = value.shape[0] // 2
        value = lax.dynamic_slice_in_dim(value, ((index // bit) % 2) * half, half, 0)
    return value


def sum_over_channels(local_sum):
    count = lax.axis_size("chan")
    bands, rows, extent = local_sum.shape
    if count & (count - 1) or count < 2 or (bands * rows) % count:
        return lax.psum(local_sum, "chan")
    chips = count // 2
    index = lax.axis_index("chan") // 2
    value = halve(local_sum.reshape(bands * rows, extent), "chan", [1])
    value = value.reshape(chips, -1, extent)
    take = lambda at: lax.dynamic_index_in_dim(value, at, 0, False)
    parts = [exchange(take(index ^ d), "chan", 2 * d) for d in range(1, chips)]
    total = sum(parts, take(index))
    sums = [total] + [exchange(total, "chan", 2 * d) for d in range(1, chips)]
    placed = []
    for place in range(chips):
        chosen = sums[0]
        for d in range(1, chips):
            chosen = jnp.where((index ^ place) == d, sums[d], chosen)
        placed.append(chosen)
    value = double(jnp.concatenate(placed, axis=0), "chan", [1])
    return value.reshape(bands, rows, extent)


def update_data(seen, data_dual, observed, live):
    count = lax.axis_size("facet")
    if count & (count - 1) or seen.shape[0] % count:
        seen = lax.psum(seen, "facet")
        return (data_dual + STEP_DATA * (seen - observed)) * live / (1.0 + STEP_DATA)
    bits = [1 << k for k in range(count.bit_length() - 1)]
    seen = halve(seen, "facet", bits)
    data_dual, observed, live = (shard_of(a, "facet", bits) for a in (data_dual, observed, live))
    fresh = (data_dual + STEP_DATA * (seen - observed)) * live / (1.0 + STEP_DATA)
    return double(fresh, "facet", bits)


def local(x_init, u_init, v_init, observed, tiles, pattern, counts, facet_bounds):
    chans, rows, extent = x_init.shape
    slots, blocks_per = pattern.shape[1:]
    tile = tiles.shape[-1]
    per_row = extent // tile
    facet = lax.axis_index("facet")
    row_start = facet * rows
    cap = chans * slots * blocks_per
    tables = [jnp.asarray(t) for t in transform_tables(extent, tile)]

    live = jnp.arange(slots, dtype=jnp.int32)[None, :] < counts[:, None]
    local_index = pattern - row_start * per_row
    keep = (local_index >= 0) & (local_index < rows * per_row) & live[:, :, None]
    keep = keep.reshape(cap)
    order = jnp.arange(cap, dtype=jnp.int32)
    ahead = jnp.sum(
        (keep[None, :] & (order[None, :] < order[:, None])).astype(jnp.int32), axis=1
    )
    packed = jnp.where(keep, local_index.reshape(cap) * cap + order, 0)
    ent = jnp.sum(
        jnp.where(keep[None, :] & (ahead[None, :] == order[:, None]), packed[None, :], 0), axis=1
    )
    kept = jnp.sum(keep.reshape(chans, -1).astype(jnp.int32), axis=1)
    edges = jnp.arange(chans + 1, dtype=jnp.int32)
    off = jnp.sum(jnp.where(edges[None, :chans] < edges[:, None], kept[None, :], 0), axis=1)

    row_ids = row_start - 1 + jnp.arange(rows + 1, dtype=jnp.int32)
    inside = (row_ids[None, :] >= facet_bounds[:, 0:1]) & (row_ids[None, :] < facet_bounds[:, 1:2])
    cover = jnp.sum(inside.astype(jnp.float32), axis=0)
    radius = (RADIUS / cover)[:, None]
    radius, radius_above = radius[1:], radius[0]

    live_float = jnp.broadcast_to(live.reshape(-1, 1, 1).astype(jnp.float32), (chans * slots, 1, 1))
    observed = observed.reshape(chans * slots, 2, tile)
    data_dual = v_init.reshape(chans * slots, 2, tile)
    tiles = tiles.reshape(cap, tile, tile)
    image, dual = x_init, u_init
    carry = shifted(u_init[:, 0, -1, :], "facet", 1)
    extra = ()
    for rounds in range(ITERS):
        image, dual, local_sum, seen, first_row, last_row, pushed_last = iteration(
            rounds == 0, rounds == ITERS - 1, tables, ent, off, data_dual, tiles, image, dual, carry, extra
        )
        half_step = STEP_PRIOR * ROOT_HALF
        pushed_last = pushed_last + half_step * shifted(first_row, "facet", -1)
        local_sum = lax.dynamic_update_slice(
            local_sum, jnp.sum(pushed_last * pushed_last, axis=0)[None, None], (0, rows - 1, 0)
        )
        total = sum_over_channels(local_sum)
        data_dual = update_data(seen, data_dual, observed, live_float)
        extra = (pushed_last, total, radius)
        if rounds + 1 < ITERS:
            above = carry + half_step * (first_row - shifted(last_row, "facet", 1))
            norms = jnp.sqrt(shifted(total[0, rows - 1 :], "facet", 1) + 1e-06)
            carry = jnp.where(facet > 0, above * jnp.minimum(1.0, radius_above / norms), 0.0)
    return (
        image,
        shrink(dual, *extra),
        data_dual.reshape(v_init.shape),
    )


def solution(mesh):
    in_specs = (
        P("chan", "facet", None),
        P("chan", None, "facet", None),
        P("chan", None, None, None),
        P("chan", None, None, None),
        P("chan", None, None, None, None),
        P("chan", None, None),
        P("chan"),
        P(),
    )
    out_specs = (
        P("chan", "facet", None),
        P("chan", None, "facet", None),
        P("chan", None, None, None),
    )
    return jax.shard_map(local, mesh=mesh, in_specs=in_specs, out_specs=out_specs, check_vma=False)
```
